32 devices in a mesh: row: 8 (over z, core), col: 4 (over y, x).
Axes of the slice: x: 2, y: 2, z: 4, core: 2. Of those that a mesh axis runs over, the one named last changes fastest.
Arguments:
- spins_up: int32 [5120, 8192], P('row', 'col'), may hold values from 0 to 1
- uniforms: float32 [2, 5120, 8192], P(None, 'row', 'col'), may hold values from 0 to 1
- moments: bfloat16 [5120, 8192], P('row', 'col'), may hold values from 0.5 to 2
- accept_bar: float32 [2], replicated, may hold values from 0.06 to 0.6, as said below
Outputs:
- spins_out: float32 [5120, 8192], P('row', 'col')
- corr: float32 [2048], P(('row', 'col'))
The draws below stay inside these ranges and needn't reach their ends.
Inputs may be any that keep to these rules, and one draw needn't show every extreme that they name: accept_bar[1] equals accept_bar[0] squared, as exp(-8 beta) and exp(-4 beta) for one inverse temperature beta of the draw.
All inputs are finite; a program needn't handle non-finite values.
Results may differ from the reference program's by a relative error of at most 0.0003.
Values may be sent and summed in bfloat16 or wider, within the bound.
No kernel may reach another device: no remote copies, remote signals or barrier semaphores. Data moves between devices by JAX's collectives and lax.ppermute only.
A program may use at most 128 MiB of HBM per device.

```python
import math
import jax
import jax.numpy as jnp
from jax import lax

ROWS = 640
CB = 2048
R = 2048
SWEEPS = 2
NR = 5120
NC = 8192


def draw_accept_bar(key, part):
    chosen = jax.random.fold_in(key, 17)
    accept_four = jax.random.uniform(chosen, (), jnp.float32, 0.25, 0.6)
    return jnp.stack([accept_four, accept_four * accept_four]).astype(jnp.float32)


def band_bits(key, length, narrow, widest, offset_top):
    width_key, phase_key, value_key = jax.random.split(key, 3)
    band_count = (length + offset_top) // narrow + 1
    widths = jax.random.randint(width_key, (band_count,), narrow, widest + 1)
    ends = jnp.cumsum(widths)
    phase = jax.random.randint(phase_key, (), 0, offset_top + 1)
    places = jnp.arange(length, dtype=jnp.int32) + phase
    band_ids = jnp.sum((places[:, None] >= ends[None, :]).astype(jnp.int32), axis=1)
    values = jax.random.randint(value_key, (band_count + 1,), 0, 2)
    return values[band_ids]


def draw_spins_up(key, part):
    base = jax.random.fold_in(key, 29)
    column_key, row_key, noise_key = jax.random.split(base, 3)
    column_narrow = max(CB // 32, 2)
    column_bits = band_bits(column_key, NC, column_narrow, 2 * CB, 2 * CB)
    row_narrow = max(ROWS // 8, 2)
    row_bits = band_bits(row_key, NR, row_narrow, 2 * ROWS, 2 * ROWS)
    noise = (jax.random.randint(noise_key, (NR, NC), 0, 10) == 0).astype(jnp.int32)
    return ((row_bits[:, None] + column_bits[None, :] + noise) % 2).astype(jnp.int32)


def shard_levels(rng, shape, shards, least, largest):
    def one(axis_at, shards_of):
        heights = jax.random.uniform(jax.random.fold_in(jax.random.fold_in(rng, 6), axis_at), (shards_of,), jnp.float32, least / len(shards), largest / len(shards))
        return jnp.repeat(jnp.exp(heights), shape[axis_at] // shards_of).reshape((-1,) + (1,) * (len(shape) - axis_at - 1))

    level = one(*shards[0])
    for cut in shards[1:]:
        level = level * one(*cut)
    return level


def setup_inputs(seed: int = 0) -> dict:
    arg_keys = jax.random.split(jax.random.key(seed), 5)
    return {
        "spins_up": draw_spins_up(jax.random.fold_in(arg_keys[4], 71), 0),
        "uniforms": jnp.clip(1.0 * jax.random.uniform(arg_keys[1], (SWEEPS, NR, NC), jnp.float32) ** shard_levels(arg_keys[1], (SWEEPS, NR, NC), ((1, 8), (2, 4)), -0.2, 0.2), 0.0, 1.0),
        "moments": jnp.clip(jnp.exp(math.log(2.0) - 1.3862944 * jax.random.uniform(arg_keys[2], (NR, NC), jnp.float32) ** shard_levels(arg_keys[2], (NR, NC), ((0, 8), (1, 4)), -0.2, 0.2)), 0.5, 2.0).astype(jnp.bfloat16),
        "accept_bar": draw_accept_bar(jax.random.fold_in(arg_keys[4], 71), 0),
    }


def update_colour(lattice, uniform_draws, accept_bar, colour):
    neighbours = jnp.roll(lattice, 1, 0) + jnp.roll(lattice, -1, 0) + jnp.roll(lattice, 1, 1) + jnp.roll(lattice, -1, 1)
    alignment = lattice * neighbours
    threshold = jnp.where(alignment > 3.0, accept_bar[1], accept_bar[0])
    row_ids = lax.broadcasted_iota(jnp.int32, lattice.shape, 0)
    col_ids = lax.broadcasted_iota(jnp.int32, lattice.shape, 1)
    coloured = (row_ids + col_ids) % 2 == colour
    flipped = coloured & ((alignment <= 0.0) | (uniform_draws < threshold))
    return jnp.where(flipped, -lattice, lattice)

def reference(spins_up, uniforms, moments, accept_bar):
    lattice = (2 * spins_up - 1).astype(jnp.float32)
    for sweep_index in range(SWEEPS):
        for colour in range(2):
            lattice = update_colour(lattice, uniforms[sweep_index], accept_bar, colour)
    weighted = (moments * lattice.astype(jnp.bfloat16)).astype(jnp.float32)
    strips = weighted.reshape(NR // ROWS, ROWS, NC)

    def strip_corr(strip_rows):
        spectrum = jnp.fft.rfft(strip_rows, axis=1)
        power_sum = spectrum.real * spectrum.real + spectrum.imag * spectrum.imag
        circular = jnp.fft.irfft(power_sum, n=NC, axis=1)
        return lax.optimization_barrier(jnp.sum(circular[:, :R], axis=0))
    partials = lax.map(strip_corr, strips)
    normaliser = 1.0 / math.sqrt(NR * NC)
    corr = (lax.optimization_barrier(jnp.sum(partials, axis=0)) * normaliser).astype(jnp.float32)
    return (lattice, corr)
```

```python
import functools
import math

import jax
import jax.numpy as jnp
from jax import lax
from jax.experimental import pallas as pl
from jax.experimental.pallas import tpu as pltpu
from jax.sharding import PartitionSpec as P

R = 2048
SWEEPS = 2
DEPTH = 32
LANES = 128
TILE = 256
PER_STEP = 2


def params(**more):
    return pltpu.CompilerParams(vmem_limit_bytes=48 << 20, **more)


def pack_kernel(bar_ref, spins_ref, draws_ref, words_ref, last_ref, first_ref):
    step = pl.program_id(0)
    planes = pl.num_programs(0) * PER_STEP
    columns = words_ref.shape[2]

    @pl.when(step == 0)
    def _():
        words_ref[...] = jnp.zeros_like(words_ref)

    for left in range(0, columns, TILE):
        lanes = pl.ds(left, TILE)
        words = [words_ref[w, :, lanes] for w in range(1 + 2 * SWEEPS)]
        for plane in range(PER_STEP):
            place = step * PER_STEP + plane + 1
            bit = jnp.int32(1) << place
            rows = pl.ds(plane * DEPTH, DEPTH)
            words[0] = words[0] | (spins_ref[rows, lanes] << place)
            for k in range(SWEEPS):
                draw = draws_ref[k, rows, lanes]
                for c in range(2):
                    word = words[1 + 2 * k + c]
                    words[1 + 2 * k + c] = jnp.where(draw < bar_ref[c], word | bit, word)
        for w, word in enumerate(words):
            words_ref[w, :, lanes] = word

    @pl.when(step == pl.num_programs(0) - 1)
    def _():
        for ref, top, place in ((last_ref, DEPTH - 8, planes), (first_ref, 0, 1)):
            bits = [
                (words_ref[w, top : top + 8, :] >> place) & 1 for w in range(1 + 2 * SWEEPS)
            ]
            ref[...] = strips(bits, True)


def strips(bits, pad):
    parts = [bits[0]] + [bits[1 + 2 * k] + 2 * bits[2 + 2 * k] for k in range(SWEEPS)]
    if pad:
        parts.append(jnp.zeros_like(parts[0]))
    return jnp.concatenate(parts, axis=0).astype(jnp.float32).astype(jnp.bfloat16)


def unstrips(ref, height):
    parts = [
        ref[k * height : (k + 1) * height, :].astype(jnp.float32).astype(jnp.int32)
        for k in range(1 + SWEEPS)
    ]
    bits = [parts[0]]
    for code in parts[1:]:
        bits += [code & 1, code >> 1]
    return bits


def spread(word):
    for shift in (4, 8, 16, 32, 64):
        word = word | pltpu.roll(word, shift, 1)
    return word


def rows_kernel(words_ref, above_ref, below_ref, joined_ref, right_ref, left_ref, *, planes):
    columns = words_ref.shape[2]
    joined_ref[...] = words_ref[...]
    above, below = unstrips(above_ref, 8), unstrips(below_ref, 8)
    for w in range(1 + 2 * SWEEPS):
        joined_ref[w, DEPTH - 8 :, :] = words_ref[w, DEPTH - 8 :, :] | above[w]
        joined_ref[w, :8, :] = words_ref[w, :8, :] | (below[w] << (planes + 1))
    lane = lax.broadcasted_iota(jnp.int32, (DEPTH, LANES), 1)
    for ref, at, held in (
        (right_ref, columns - LANES, lane >= LANES - 4),
        (left_ref, 0, lane < 4),
    ):
        bits = []
        for w in range(1 + 2 * SWEEPS):
            edge = jnp.where(held, joined_ref[w, :, at : at + LANES], 0)
            bits.append((spread(edge) >> (lane // 4)) & 1)
        ref[...] = strips(bits, False)


def sweeps_of(words):
    spins = words[0]
    width = spins.shape[1]
    row = lax.broadcasted_iota(jnp.int32, spins.shape, 0)
    parity = (row + lax.broadcasted_iota(jnp.int32, spins.shape, 1)) & 1
    for k in range(SWEEPS):
        for colour in range(2):
            up = pltpu.roll(spins, 1, 0)
            up = jnp.where(row == 0, up << 1, up)
            down = pltpu.roll(spins, DEPTH - 1, 0)
            down = jnp.where(row == DEPTH - 1, down >> 1, down)
            a, b = up ^ spins, down ^ spins
            c, d = pltpu.roll(spins, 1, 1) ^ spins, pltpu.roll(spins, width - 1, 1) ^ spins
            either, other = a | b, c | d
            some = either | other
            several = (a & b) | (c & d) | (either & other)
            flips = several | (some & words[1 + 2 * k]) | (words[2 + 2 * k] & ~some)
            spins = jnp.where(parity == colour, spins ^ flips, spins)
    return spins


def sweep_kernel(words_ref, before_ref, after_ref, spins_ref):
    columns = words_ref.shape[2]
    lane = lax.broadcasted_iota(jnp.int32, (DEPTH, LANES), 1)
    before, after = unstrips(before_ref, DEPTH), unstrips(after_ref, DEPTH)
    words = [
        jnp.concatenate(
            [
                spread(before[w] << (lane // 4)),
                words_ref[w],
                spread(after[w] << (lane // 4)),
            ],
            axis=1,
        )
        for w in range(1 + 2 * SWEEPS)
    ]
    spins_ref[...] = sweeps_of(words)[:, LANES : LANES + columns]


def weigh_kernel(half_ref, spins_ref, moments_ref, out_ref):
    first = (half_ref[0] * pl.num_programs(0) + pl.program_id(0)) * PER_STEP + 1
    for plane in range(PER_STEP):
        bit = jnp.int32(1) << (first + plane)
        rows = pl.ds(plane * DEPTH, DEPTH)
        for t in range(out_ref.shape[0]):
            lanes = pl.ds(t * TILE, TILE)
            size = moments_ref[rows, lanes].astype(jnp.float32)
            up = (spins_ref[:, lanes] & bit) != 0
            out_ref[t, rows, :] = jnp.where(up, size, -size).astype(jnp.bfloat16)


def spell_kernel(spins_ref, out_ref):
    first = pl.program_id(0) * PER_STEP + 1
    for plane in range(PER_STEP):
        bit = jnp.int32(1) << (first + plane)
        rows = pl.ds(plane * DEPTH, DEPTH)
        out_ref[rows, :] = jnp.where((spins_ref[...] & bit) != 0, 1.0, -1.0)


def gram(left, right):
    depth = left.shape[0] * left.shape[1]
    return lax.dot_general(
        left.reshape(depth, TILE),
        right.reshape(depth, TILE),
        (((0,), (0,)), ((), ())),
        preferred_element_type=jnp.float32,
    )


def fold(sums_ref):
    width = R + LANES
    value = sums_ref[:LANES, :width] + sums_ref[LANES:, LANES : LANES + width]
    height = LANES // 2
    while height >= 8:
        value = value[:height] + pltpu.roll(value[height:], width - height, 1)
        height //= 2
    return value


def own_kernel(first_ref, second_ref, out_ref, sums_ref):
    tiles = first_ref.shape[0]
    for n in range(tiles):
        sums_ref[:, n * TILE : (n + 1) * TILE] = gram(
            first_ref[: tiles - n], first_ref[n:]
        ) + gram(second_ref[: tiles - n], second_ref[n:])
    sums_ref[:, tiles * TILE :] = jnp.zeros((TILE, TILE), jnp.float32)
    out_ref[...] = fold(sums_ref)


def next_kernel(odd_ref, own_ref, mid_ref, far_ref, base_ref, out_ref, sums_ref, ends_ref, sems):
    odd = odd_ref[0]
    copies = (
        pltpu.make_async_copy(own_ref, ends_ref.at[odd], sems.at[0]),
        pltpu.make_async_copy(far_ref, ends_ref.at[1 - odd], sems.at[1]),
    )
    for copy in copies:
        copy.start()
    for copy in copies:
        copy.wait()
    tiles = mid_ref.shape[0]
    sums_ref[:, :TILE] = jnp.zeros((TILE, TILE), jnp.float32)
    for n in range(1, tiles + 1):
        sums_ref[:, n * TILE : (n + 1) * TILE] = gram(
            ends_ref[0, tiles - n :], mid_ref[:n]
        ) + gram(mid_ref[tiles - n :], ends_ref[1, :n])
    value = fold(sums_ref) + base_ref[...]
    for height in (4, 2, 1):
        value = value + pltpu.roll(pltpu.roll(value, value.shape[1] - height, 1), 8 - height, 0)
    out_ref[...] = value[:1, :R]


def on_device(spins_up, uniforms, moments, accept_bar):
    rows, columns = spins_up.shape
    planes, tiles = rows // DEPTH, columns // TILE
    half_rows = rows // 2
    row_devices, col_devices = lax.axis_size("row"), lax.axis_size("col")
    assert columns == R and col_devices % 2 == 0 and planes + 2 <= 26
    count = 1 + 2 * SWEEPS
    block = PER_STEP * DEPTH
    vmem = pl.BlockSpec(memory_space=pltpu.VMEM)
    smem = pl.BlockSpec(memory_space=pltpu.SMEM)
    anywhere = pl.BlockSpec(memory_space=pl.ANY)
    strip_shape = jax.ShapeDtypeStruct((8 * (2 + SWEEPS), columns), jnp.bfloat16)
    edge_shape = jax.ShapeDtypeStruct((DEPTH * (1 + SWEEPS), LANES), jnp.bfloat16)
    words_shape = jax.ShapeDtypeStruct((count, DEPTH, columns), jnp.int32)

    words, last, leading = pl.pallas_call(
        pack_kernel,
        grid=(rows // block,),
        in_specs=[
            smem,
            pl.BlockSpec((block, columns), lambda i: (i, 0)),
            pl.BlockSpec((SWEEPS, block, columns), lambda i: (0, i, 0)),
        ],
        out_specs=[
            pl.BlockSpec(words_shape.shape, lambda i: (0, 0, 0)),
            pl.BlockSpec(strip_shape.shape, lambda i: (0, 0)),
            pl.BlockSpec(strip_shape.shape, lambda i: (0, 0)),
        ],
        out_shape=[words_shape, strip_shape, strip_shape],
        compiler_params=params(),
        name="pack",
    )(accept_bar, spins_up, uniforms)

    def ring(size, step):
        return [(i, (i + step) % size) for i in range(size)]

    above = lax.ppermute(last, "row", ring(row_devices, 1))
    below = lax.ppermute(leading, "row", ring(row_devices, -1))
    joined, right, left = pl.pallas_call(
        functools.partial(rows_kernel, planes=planes),
        in_specs=[vmem] * 3,
        out_specs=[vmem] * 3,
        out_shape=[words_shape, edge_shape, edge_shape],
        compiler_params=params(),
        name="rows",
    )(words, above, below)
    before = lax.ppermute(right, "col", ring(col_devices, 1))
    after = lax.ppermute(left, "col", ring(col_devices, -1))
    spins = pl.pallas_call(
        sweep_kernel,
        in_specs=[vmem] * 3,
        out_specs=vmem,
        out_shape=jax.ShapeDtypeStruct((DEPTH, columns), jnp.int32),
        compiler_params=params(),
        name="sweep",
    )(joined, before, after)

    odd = lax.axis_index("col") % 2

    def weigh(half):
        steps = half_rows // block
        return pl.pallas_call(
            weigh_kernel,
            grid_spec=pltpu.PrefetchScalarGridSpec(
                num_scalar_prefetch=1,
                grid=(steps,),
                in_specs=[
                    pl.BlockSpec((DEPTH, columns), lambda i, h: (0, 0)),
                    pl.BlockSpec((block, columns), lambda i, h: (h[0] * steps + i, 0)),
                ],
                out_specs=pl.BlockSpec((tiles, block, TILE), lambda i, h: (0, i, 0)),
            ),
            out_shape=jax.ShapeDtypeStruct((tiles, half_rows, TILE), jnp.bfloat16),
            compiler_params=params(),
            name="weigh",
        )(half.reshape(1), spins, moments)

    given, kept = weigh(1 - odd), weigh(odd)
    mid = lax.ppermute(given, "col", [(i, i ^ 1) for i in range(col_devices)])
    far = lax.ppermute(
        kept, "col", [(i, (i - 2 + 4 * (i % 2)) % col_devices) for i in range(col_devices)]
    )
    spins_out = pl.pallas_call(
        spell_kernel,
        grid=(rows // block,),
        in_specs=[pl.BlockSpec((DEPTH, columns), lambda i: (0, 0))],
        out_specs=pl.BlockSpec((block, columns), lambda i: (i, 0)),
        out_shape=jax.ShapeDtypeStruct((rows, columns), jnp.float32),
        compiler_params=params(),
        cost_estimate=pl.CostEstimate(
            flops=rows * columns, bytes_accessed=4 * rows * columns, transcendentals=0
        ),
        name="spell",
    )(spins)
    sums = pltpu.VMEM((TILE, R + TILE), jnp.float32)
    base = pl.pallas_call(
        own_kernel,
        in_specs=[vmem] * 2,
        out_specs=vmem,
        out_shape=jax.ShapeDtypeStruct((8, R + LANES), jnp.float32),
        scratch_shapes=[sums],
        compiler_params=params(),
        cost_estimate=pl.CostEstimate(
            flops=rows * columns * columns, bytes_accessed=2 * rows * columns, transcendentals=0
        ),
        name="own",
    )(given, kept)
    partial_sums = pl.pallas_call(
        next_kernel,
        in_specs=[smem, anywhere, vmem, anywhere, vmem],
        out_specs=vmem,
        out_shape=jax.ShapeDtypeStruct((1, R), jnp.float32),
        scratch_shapes=[
            sums,
            pltpu.VMEM((2, tiles, half_rows, TILE), jnp.bfloat16),
            pltpu.SemaphoreType.DMA((2,)),
        ],
        compiler_params=params(),
        name="next",
    )(odd.reshape(1), kept, mid, far, base)
    normaliser = 1.0 / math.sqrt(rows * row_devices * columns * col_devices)
    devices = row_devices * col_devices
    shares = lax.all_to_all(
        partial_sums.reshape(devices, R // devices), ("row", "col"), 0, 0, tiled=True
    )
    return spins_out, jnp.sum(shares, axis=0) * normaliser


def solution(mesh):
    placed = (P("row", "col"), P(None, "row", "col"), P("row", "col"), P())
    return jax.shard_map(
        on_device,
        mesh=mesh,
        in_specs=placed,
        out_specs=(P("row", "col"), P(("row", "col"))),
        check_vma=False,
    )
```

```python
import functools
import math

import jax
import jax.numpy as jnp
from jax import lax
from jax.experimental import pallas as pl
from jax.experimental.pallas import tpu as pltpu
from jax.sharding import PartitionSpec as P

R = 2048
SWEEPS = 2
DEPTH = 32
LANES = 128
TILE = 256
PER_STEP = 2
MIDDLE = 4
WORDS = 1 + 2 * SWEEPS


def params(**more):
    return pltpu.CompilerParams(vmem_limit_bytes=48 << 20, **more)


def fetch(step, spins_hbm, draws_hbm, spins_buf, draws_buf, sems, row, at, count):
    copies = [
        pltpu.make_async_copy(
            spins_hbm.at[pl.ds(row, count)], spins_buf.at[pl.ds(at, count)], sems.at[step, 0]
        )
    ]
    for k in range(SWEEPS):
        copies.append(
            pltpu.make_async_copy(
                draws_hbm.at[k, pl.ds(row, count)],
                draws_buf.at[k, pl.ds(at, count)],
                sems.at[step, 1 + k],
            )
        )
    return copies


def pack(bar_ref, words_ref, spins_buf, draws_buf, planes, at, fresh):
    columns = words_ref.shape[2]
    for left in range(0, columns, TILE):
        lanes = pl.ds(left, TILE)
        if fresh:
            words = [jnp.zeros((DEPTH, TILE), jnp.int32)] * WORDS
        else:
            words = [words_ref[w, :, lanes] for w in range(WORDS)]
        for i, plane in enumerate(planes):
            bit = 1 << (plane + 1)
            rows = pl.ds(at + i * DEPTH, DEPTH)
            words[0] = words[0] | (spins_buf[rows, lanes] << (plane + 1))
            for k in range(SWEEPS):
                draw = draws_buf[k, rows, lanes]
                for c in range(2):
                    word = words[1 + 2 * k + c]
                    words[1 + 2 * k + c] = jnp.where(draw < bar_ref[c], word | bit, word)
        for w, word in enumerate(words):
            words_ref[w, :, lanes] = word


def groups_of(planes, size):
    return [planes[i : i + size] for i in range(0, len(planes), size)]


def strips(parts):
    return jnp.concatenate(parts, axis=0).astype(jnp.float32).astype(jnp.bfloat16)


def codes(bits):
    return [bits[0]] + [bits[1 + 2 * k] + 2 * bits[2 + 2 * k] for k in range(SWEEPS)]


def unstrips(ref, height):
    parts = [
        ref[k * height : (k + 1) * height, :].astype(jnp.float32).astype(jnp.int32)
        for k in range(1 + SWEEPS)
    ]
    bits = [parts[0]]
    for code in parts[1:]:
        bits += [code & 1, code >> 1]
    return bits


def spread(word):
    for shift in (4, 8, 16, 32, 64):
        word = word | pltpu.roll(word, shift, 1)
    return word


def sweeps_of(words):
    spins = words[0]
    width = spins.shape[1]
    row = lax.broadcasted_iota(jnp.int32, spins.shape, 0)
    parity = (row + lax.broadcasted_iota(jnp.int32, spins.shape, 1)) & 1
    for k in range(SWEEPS):
        for colour in range(2):
            up = pltpu.roll(spins, 1, 0)
            up = jnp.where(row == 0, up << 1, up)
            down = pltpu.roll(spins, DEPTH - 1, 0)
            down = jnp.where(row == DEPTH - 1, down >> 1, down)
            a, b = up ^ spins, down ^ spins
            c, d = pltpu.roll(spins, 1, 1) ^ spins, pltpu.roll(spins, width - 1, 1) ^ spins
            either, other = a | b, c | d
            some = either | other
            several = (a & b) | (c & d) | (either & other)
            flips = several | (some & words[1 + 2 * k]) | (words[2 + 2 * k] & ~some)
            spins = jnp.where(parity == colour, spins ^ flips, spins)
    return spins


def weigh(spins, moments, plane):
    up = (spins & (jnp.int32(1) << (plane + 1))) != 0
    size = moments.astype(jnp.float32)
    return jnp.where(up, size, -size).astype(jnp.bfloat16)


def middle_kernel(
    odd_ref,
    bar_ref,
    spins_hbm,
    draws_hbm,
    moments_hbm,
    words_ref,
    last_ref,
    first_ref,
    given_ref,
    kept_ref,
    spins_buf,
    draws_buf,
    edge_spins,
    edge_draws,
    moments_buf,
    final_ref,
    sems,
    edge_sems,
):
    rows, columns = spins_hbm.shape
    half = rows // DEPTH // 2
    planes = list(range(half - MIDDLE - 1, half + MIDDLE + 1))
    top = planes[0] * DEPTH
    groups = groups_of(planes, PER_STEP)
    size = PER_STEP * DEPTH
    edges = [
        fetch(s, spins_hbm, draws_hbm, edge_spins, edge_draws, edge_sems, row, 8 * s, 8)
        for s, row in enumerate((rows - 8, 0))
    ]
    copies = [
        fetch(
            g,
            spins_hbm,
            draws_hbm,
            spins_buf,
            draws_buf,
            sems,
            top + g * size,
            g * size,
            len(group) * DEPTH,
        )
        for g, group in enumerate(groups)
    ]
    weights = pltpu.make_async_copy(
        moments_hbm.at[pl.ds((half - MIDDLE) * DEPTH, 2 * MIDDLE * DEPTH)],
        moments_buf,
        edge_sems.at[2, 0],
    )
    for copy in sum(edges + copies, []) + [weights]:
        copy.start()
    for s, ref in enumerate((last_ref, first_ref)):
        for copy in edges[s]:
            copy.wait()
        parts = [edge_spins[8 * s : 8 * s + 8, :]]
        for k in range(SWEEPS):
            draw = edge_draws[k, 8 * s : 8 * s + 8, :]
            one = (draw < bar_ref[0]).astype(jnp.int32)
            parts.append(one + 2 * (draw < bar_ref[1]).astype(jnp.int32))
        ref[...] = strips(parts + [jnp.zeros_like(parts[0])])
    for g, group in enumerate(groups):
        for copy in copies[g]:
            copy.wait()
        pack(bar_ref, words_ref, spins_buf, draws_buf, group, g * size, g == 0)
    inner = slice(LANES, columns - LANES)
    final_ref[:, inner] = sweeps_of([words_ref[w, :, inner] for w in range(WORDS)])
    weights.wait()
    for ref, lower in ((given_ref, 1 - odd_ref[0]), (kept_ref, odd_ref[0])):
        for i in range(MIDDLE):
            plane = half - MIDDLE + MIDDLE * lower + i
            at = pl.ds(pl.multiple_of((MIDDLE * lower + i) * DEPTH, DEPTH), DEPTH)
            for t in range(ref.shape[0]):
                lanes = pl.ds((t + 1) * TILE, TILE)
                ref[t, i * DEPTH : (i + 1) * DEPTH, :] = weigh(
                    final_ref[:, lanes], moments_buf[at, lanes], plane
                )


def outer_kernel(bar_ref, spins_hbm, draws_hbm, middle_ref, words_ref, spins_buf, draws_buf, sems):
    planes = spins_hbm.shape[0] // DEPTH
    side = planes // 2 - MIDDLE - 1
    outer = list(range(side)) + list(range(planes - side, planes))
    copies = []
    for g, plane in enumerate(outer):
        copies.append(
            fetch(
                g,
                spins_hbm,
                draws_hbm,
                spins_buf,
                draws_buf,
                sems,
                plane * DEPTH,
                g * DEPTH,
                DEPTH,
            )
        )
        for copy in copies[-1]:
            copy.start()
    words_ref[...] = middle_ref[...]
    for g in range(0, len(outer), PER_STEP):
        group = outer[g : g + PER_STEP]
        for copy in sum(copies[g : g + PER_STEP], []):
            copy.wait()
        pack(bar_ref, words_ref, spins_buf, draws_buf, group, g * DEPTH, False)


def inner_kernel(
    odd_ref,
    words_ref,
    above_ref,
    below_ref,
    moments_hbm,
    spins_ref,
    sides_ref,
    right_ref,
    left_ref,
    given_ref,
    kept_ref,
    joined_ref,
    moments_buf,
    sems,
):
    rows, columns = moments_hbm.shape
    planes = rows // DEPTH
    side = planes // 2 - MIDDLE
    weights = [
        pltpu.make_async_copy(
            moments_hbm.at[pl.ds(row, side * DEPTH)], moments_buf.at[s], sems.at[s]
        )
        for s, row in enumerate((0, rows - side * DEPTH))
    ]
    for copy in weights:
        copy.start()
    above, below = unstrips(above_ref, 8), unstrips(below_ref, 8)
    joined_ref[...] = words_ref[...]
    for w in range(WORDS):
        joined_ref[w, DEPTH - 8 :, :] = words_ref[w, DEPTH - 8 :, :] | above[w]
        joined_ref[w, :8, :] = words_ref[w, :8, :] | (below[w] << (planes + 1))
    lane = lax.broadcasted_iota(jnp.int32, (DEPTH, LANES), 1)
    for ref, at, held in (
        (right_ref, columns - LANES, lane >= LANES - 4),
        (left_ref, 0, lane < 4),
    ):
        bits = []
        for w in range(WORDS):
            edge = jnp.where(held, joined_ref[w, :, at : at + LANES], 0)
            bits.append((spread(edge) >> (lane // 4)) & 1)
        ref[...] = strips(codes(bits))
    reach = TILE + LANES
    sides_ref[:, :, :reach] = joined_ref[:, :, :reach]
    sides_ref[:, :, reach:] = joined_ref[:, :, columns - reach :]
    inner = slice(LANES, columns - LANES)
    spins_ref[:, :LANES] = jnp.zeros((DEPTH, LANES), jnp.int32)
    spins_ref[:, columns - LANES :] = jnp.zeros((DEPTH, LANES), jnp.int32)
    spins_ref[:, inner] = sweeps_of([joined_ref[w, :, inner] for w in range(WORDS)])
    for copy in weights:
        copy.wait()
    for ref, lower in ((given_ref, 1 - odd_ref[0]), (kept_ref, odd_ref[0])):
        for i in range(side):
            plane = (planes - side) * lower + i
            for t in range(ref.shape[0]):
                lanes = pl.ds((t + 1) * TILE, TILE)
                ref[t, i * DEPTH : (i + 1) * DEPTH, :] = weigh(
                    spins_ref[:, lanes],
                    moments_buf[lower, i * DEPTH : (i + 1) * DEPTH, lanes],
                    plane,
                )


def side_kernel(
    odd_ref,
    sides_ref,
    before_ref,
    after_ref,
    moments_hbm,
    spins_ref,
    given_ref,
    kept_ref,
    moments_buf,
    final_ref,
    sems,
):
    rows, columns = moments_hbm.shape
    half = rows // DEPTH // 2
    weights = [
        pltpu.make_async_copy(
            moments_hbm.at[:, pl.ds(at, TILE)], moments_buf.at[s], sems.at[s]
        )
        for s, at in enumerate((0, columns - TILE))
    ]
    for copy in weights:
        copy.start()
    lane = lax.broadcasted_iota(jnp.int32, (DEPTH, LANES), 1)
    before, after = unstrips(before_ref, DEPTH), unstrips(after_ref, DEPTH)
    words = [
        jnp.concatenate(
            [spread(before[w] << (lane // 4)), sides_ref[w], spread(after[w] << (lane // 4))],
            axis=1,
        )
        for w in range(WORDS)
    ]
    updated = sweeps_of(words)
    width = updated.shape[1]
    final_ref[0] = updated[:, LANES : LANES + TILE]
    final_ref[1] = updated[:, width - LANES - TILE : width - LANES]
    spins_ref[...] = final_ref[...]
    for copy in weights:
        copy.wait()
    for ref, lower in ((given_ref, 1 - odd_ref[0]), (kept_ref, odd_ref[0])):
        for i in range(half):
            plane = i + lower * (half + MIDDLE if i < half - MIDDLE else MIDDLE)
            at = pl.ds(pl.multiple_of(plane * DEPTH, DEPTH), DEPTH)
            for s in range(2):
                ref[s, i * DEPTH : (i + 1) * DEPTH, :] = weigh(
                    final_ref[s], moments_buf[s, at, :], plane
                )


def spell_kernel(spins_ref, sides_ref, out_ref):
    columns = out_ref.shape[1]
    first = pl.program_id(0) * PER_STEP + 1
    for plane in range(PER_STEP):
        bit = jnp.int32(1) << (first + plane)
        rows = pl.ds(plane * DEPTH, DEPTH)
        for left in range(0, columns, TILE):
            if left == 0:
                word = sides_ref[0]
            elif left == columns - TILE:
                word = sides_ref[1]
            else:
                word = spins_ref[:, left : left + TILE]
            out_ref[rows, left : left + TILE] = jnp.where((word & bit) != 0, 1.0, -1.0)


def gram(left, right):
    return lax.dot_general(
        left, right, (((0,), (0,)), ((), ())), preferred_element_type=jnp.float32
    )


def stack(refs, first, last):
    return jnp.concatenate(
        [ref[first:last].reshape((last - first) * ref.shape[1], TILE) for ref in refs], axis=0
    )


def fold(sums_ref):
    width = R + LANES
    value = sums_ref[:LANES, :width] + sums_ref[LANES:, LANES : LANES + width]
    height = LANES // 2
    while height >= 8:
        value = value[:height] + pltpu.roll(value[height:], width - height, 1)
        height //= 2
    return value


def own_kernel(*refs):
    parts, (out_ref, sums_ref, full_ref, sems) = refs[:-4], refs[-4:]
    copies = []
    for h in range(2):
        low, high, ends = parts[3 * h : 3 * h + 3]
        split = low.shape[1]
        full = full_ref.at[h]
        tiles = full_ref.shape[1]
        for source, target in (
            (low, full.at[pl.ds(1, tiles - 2), pl.ds(0, split)]),
            (high, full.at[pl.ds(1, tiles - 2), pl.ds(split, high.shape[1])]),
            (ends.at[0], full.at[0]),
            (ends.at[1], full.at[tiles - 1]),
        ):
            copies.append(pltpu.make_async_copy(source, target, sems.at[len(copies)]))
            copies[-1].start()
    for copy in copies:
        copy.wait()
    for n in range(tiles):
        sums_ref[:, n * TILE : (n + 1) * TILE] = sum(
            gram(stack([full_ref.at[h]], 0, tiles - n), stack([full_ref.at[h]], n, tiles))
            for h in range(2)
        )
    sums_ref[:, tiles * TILE :] = jnp.zeros((TILE, TILE), jnp.float32)
    out_ref[...] = fold(sums_ref)


def by_side(odd_ref, own, mid, far, run):
    @pl.when(odd_ref[0] == 0)
    def _():
        run(((own, mid), (mid, far)))

    @pl.when(odd_ref[0] == 1)
    def _():
        run(((far, mid), (mid, own)))


def early_kernel(odd_ref, *refs):
    (base_ref, out_ref, sums_ref) = refs[-3:]
    tiles = refs[0].shape[0]
    sums_ref[:, : 3 * TILE] = jnp.zeros((TILE, 3 * TILE), jnp.float32)

    def run(pairs):
        for n in range(1, tiles + 1):
            sums_ref[:, (n + 2) * TILE : (n + 3) * TILE] = sum(
                gram(stack(left, tiles - n, tiles), stack(right, 0, n)) for left, right in pairs
            )

    by_side(odd_ref, refs[0:2], refs[2:4], refs[4:6], run)
    out_ref[...] = fold(sums_ref) + base_ref[...]


def late_kernel(odd_ref, *refs):
    (base_ref, out_ref, sums_ref) = refs[-3:]
    tiles = refs[0].shape[0] + 2
    sums_ref[:, :TILE] = jnp.zeros((TILE, TILE), jnp.float32)

    def tile(block, t):
        low, high, ends = block
        if t in (0, tiles - 1):
            return ends[min(t, 1)]
        return stack([low, high], t - 1, t)

    def run(pairs):
        for n in range(1, tiles + 1):
            places = [(tiles - 1, n - 1)] + ([(tiles - n, 0)] if n > 1 else [])
            sums_ref[:, n * TILE : (n + 1) * TILE] = sum(
                gram(
                    jnp.concatenate([tile(left, t) for t, _ in places], axis=0),
                    jnp.concatenate([tile(right, q) for _, q in places], axis=0),
                )
                for left, right in pairs
            )

    by_side(odd_ref, refs[0:3], refs[3:6], refs[6:9], run)
    value = fold(sums_ref) + base_ref[...]
    for height in (4, 2, 1):
        value = value + pltpu.roll(pltpu.roll(value, value.shape[1] - height, 1), 8 - height, 0)
    share = out_ref.shape[2]
    for d in range(out_ref.shape[0]):
        out_ref[d] = value[:1, d * share : (d + 1) * share]


def on_device(spins_up, uniforms, moments, accept_bar):
    rows, columns = spins_up.shape
    planes, tiles = rows // DEPTH, columns // TILE
    half_rows, half = rows // 2, planes // 2
    row_devices, col_devices = lax.axis_size("row"), lax.axis_size("col")
    devices = row_devices * col_devices
    assert columns == R and col_devices % 2 == 0 and planes % 2 == 0 and planes + 2 <= 26
    vmem = pl.BlockSpec(memory_space=pltpu.VMEM)
    smem = pl.BlockSpec(memory_space=pltpu.SMEM)
    anywhere = pl.BlockSpec(memory_space=pl.ANY)
    strip = jax.ShapeDtypeStruct((8 * (2 + SWEEPS), columns), jnp.bfloat16)
    edge = jax.ShapeDtypeStruct((DEPTH * (1 + SWEEPS), LANES), jnp.bfloat16)
    words_shape = jax.ShapeDtypeStruct((WORDS, DEPTH, columns), jnp.int32)
    dma = pltpu.SemaphoreType.DMA
    odd = (lax.axis_index("col") % 2).reshape(1)

    def message(count, height):
        return jax.ShapeDtypeStruct((count, height, TILE), jnp.bfloat16)

    def ring(size, step):
        return [(i, (i + step) % size) for i in range(size)]

    def exchange(given, kept):
        mid = lax.ppermute(given, "col", [(i, i ^ 1) for i in range(col_devices)])
        far = lax.ppermute(
            kept, "col", [(i, (i - 2 + 4 * (i % 2)) % col_devices) for i in range(col_devices)]
        )
        return mid, far

    def call(kernel, name, specs, shapes, scratch, flops, moved, *operands):
        return pl.pallas_call(
            kernel,
            in_specs=specs,
            out_specs=jax.tree.map(lambda _: vmem, shapes),
            out_shape=shapes,
            scratch_shapes=scratch,
            compiler_params=params(),
            cost_estimate=pl.CostEstimate(flops=flops, bytes_accessed=moved, transcendentals=0),
            name=name,
        )(*operands)

    packed = (2 * MIDDLE + 2) * DEPTH
    middle = message(tiles - 2, MIDDLE * DEPTH)
    words, last, leading, given, kept = call(
        middle_kernel,
        "middle",
        [smem, smem, anywhere, anywhere, anywhere],
        [words_shape, strip, strip, middle, middle],
        [
            pltpu.VMEM((packed, columns), jnp.int32),
            pltpu.VMEM((SWEEPS, packed, columns), jnp.float32),
            pltpu.VMEM((16, columns), jnp.int32),
            pltpu.VMEM((SWEEPS, 16, columns), jnp.float32),
            pltpu.VMEM((2 * MIDDLE * DEPTH, columns), jnp.bfloat16),
            pltpu.VMEM((DEPTH, columns), jnp.int32),
            dma((pl.cdiv(2 * MIDDLE + 2, PER_STEP), 1 + SWEEPS)),
            dma((3, 1 + SWEEPS)),
        ],
        40 * packed * columns,
        4 * (1 + SWEEPS) * packed * columns,
        odd,
        accept_bar,
        spins_up,
        uniforms,
        moments,
    )
    own = [given, kept]
    got = [*exchange(given, kept)]
    above = lax.ppermute(last, "row", ring(row_devices, 1))
    below = lax.ppermute(leading, "row", ring(row_devices, -1))

    remaining = rows - packed
    words = call(
        outer_kernel,
        "outer",
        [smem, anywhere, anywhere, vmem],
        words_shape,
        [
            pltpu.VMEM((remaining, columns), jnp.int32),
            pltpu.VMEM((SWEEPS, remaining, columns), jnp.float32),
            dma((remaining // DEPTH, 1 + SWEEPS)),
        ],
        40 * remaining * columns,
        4 * (1 + SWEEPS) * remaining * columns,
        accept_bar,
        spins_up,
        uniforms,
        words,
    )
    side = half - MIDDLE
    low = message(tiles - 2, side * DEPTH)
    reach = 2 * (TILE + LANES)
    spins, sides, right, left, given, kept = call(
        inner_kernel,
        "inner",
        [smem, vmem, vmem, vmem, anywhere],
        [
            jax.ShapeDtypeStruct((DEPTH, columns), jnp.int32),
            jax.ShapeDtypeStruct((WORDS, DEPTH, reach), jnp.int32),
            edge,
            edge,
            low,
            low,
        ],
        [
            pltpu.VMEM(words_shape.shape, jnp.int32),
            pltpu.VMEM((2, side * DEPTH, columns), jnp.bfloat16),
            dma((2,)),
        ],
        40 * rows * columns,
        4 * rows * columns,
        odd,
        words,
        above,
        below,
        moments,
    )
    own = [given, own[0], kept, own[1]]
    mid, far = exchange(given, kept)
    got = [mid, got[0], far, got[1]]
    before = lax.ppermute(right, "col", ring(col_devices, 1))
    after = lax.ppermute(left, "col", ring(col_devices, -1))
    ends = message(2, half_rows)
    side_spins, given, kept = call(
        side_kernel,
        "side",
        [smem, vmem, vmem, vmem, anywhere],
        [jax.ShapeDtypeStruct((2, DEPTH, TILE), jnp.int32), ends, ends],
        [
            pltpu.VMEM((2, rows, TILE), jnp.bfloat16),
            pltpu.VMEM((2, DEPTH, TILE), jnp.int32),
            dma((2,)),
        ],
        10 * rows * columns,
        rows * columns,
        odd,
        sides,
        before,
        after,
        moments,
    )
    own = [own[0], own[1], given, own[2], own[3], kept]
    mid, far = exchange(given, kept)

    spins_out = pl.pallas_call(
        spell_kernel,
        grid=(rows // (PER_STEP * DEPTH),),
        in_specs=[
            pl.BlockSpec((DEPTH, columns), lambda i: (0, 0)),
            pl.BlockSpec((2, DEPTH, TILE), lambda i: (0, 0, 0)),
        ],
        out_specs=pl.BlockSpec((PER_STEP * DEPTH, columns), lambda i: (i, 0)),
        out_shape=jax.ShapeDtypeStruct((rows, columns), jnp.float32),
        compiler_params=params(),
        cost_estimate=pl.CostEstimate(
            flops=rows * columns, bytes_accessed=4 * rows * columns, transcendentals=0
        ),
        name="spell",
    )(spins, side_spins)
    sums = pltpu.VMEM((TILE, R + TILE), jnp.float32)
    folded = jax.ShapeDtypeStruct((8, R + LANES), jnp.float32)
    work = rows * columns * columns
    base = call(
        own_kernel,
        "own",
        [vmem] * 6,
        folded,
        [sums, pltpu.VMEM((2, tiles, half_rows, TILE), jnp.bfloat16), dma((8,))],
        work,
        2 * rows * columns,
        *own,
    )
    base = call(
        early_kernel,
        "early",
        [smem] + [vmem] * 7,
        folded,
        [sums],
        work // 2,
        2 * rows * columns,
        odd,
        own[3],
        own[4],
        *got,
        base,
    )
    partial_sums = call(
        late_kernel,
        "late",
        [smem] + [vmem] * 10,
        jax.ShapeDtypeStruct((devices, 1, R // devices), jnp.float32),
        [sums],
        work // 2,
        2 * rows * columns,
        odd,
        own[3],
        own[4],
        own[5],
        got[0],
        got[1],
        mid,
        got[2],
        got[3],
        far,
        base,
    )
    normaliser = 1.0 / math.sqrt(rows * row_devices * columns * col_devices)
    shares = lax.all_to_all(partial_sums, ("row", "col"), 0, 0, tiled=True)
    return spins_out, jnp.sum(shares, axis=(0, 1)) * normaliser


def solution(mesh):
    placed = (P("row", "col"), P(None, "row", "col"), P("row", "col"), P())
    return jax.shard_map(
        on_device,
        mesh=mesh,
        in_specs=placed,
        out_specs=(P("row", "col"), P(("row", "col"))),
        check_vma=False,
    )
```

```python
import math

import jax
import jax.numpy as jnp
from jax import lax
from jax.experimental import pallas as pl
from jax.experimental.pallas import tpu as pltpu
from jax.sharding import PartitionSpec as P

R = 2048
SWEEPS = 2
DEPTH = 32
LANES = 128
TILE = 256
PER_STEP = 2
MIDDLE = 7
WORDS = 1 + 2 * SWEEPS


def params(**more):
    return pltpu.CompilerParams(vmem_limit_bytes=48 << 20, **more)


def fetch(step, spins_hbm, draws_hbm, spins_buf, draws_buf, sems, row, at, count):
    copies = [
        pltpu.make_async_copy(
            spins_hbm.at[pl.ds(row, count)], spins_buf.at[pl.ds(at, count)], sems.at[step, 0]
        )
    ]
    for k in range(SWEEPS):
        copies.append(
            pltpu.make_async_copy(
                draws_hbm.at[k, pl.ds(row, count)],
                draws_buf.at[k, pl.ds(at, count)],
                sems.at[step, 1 + k],
            )
        )
    return copies


def pack(bar_ref, words_ref, spins_buf, draws_buf, planes, at, fresh):
    columns = words_ref.shape[2]
    for left in range(0, columns, TILE):
        lanes = pl.ds(left, TILE)
        if fresh:
            words = [jnp.zeros((DEPTH, TILE), jnp.int32)] * WORDS
        else:
            words = [words_ref[w, :, lanes] for w in range(WORDS)]
        for i, plane in enumerate(planes):
            bit = 1 << (plane + 1)
            rows = pl.ds(at + i * DEPTH, DEPTH)
            words[0] = words[0] | (spins_buf[rows, lanes] << (plane + 1))
            for k in range(SWEEPS):
                draw = draws_buf[k, rows, lanes]
                for c in range(2):
                    word = words[1 + 2 * k + c]
                    words[1 + 2 * k + c] = jnp.where(draw < bar_ref[c], word | bit, word)
        for w, word in enumerate(words):
            words_ref[w, :, lanes] = word


def groups_of(planes, size):
    return [planes[i : i + size] for i in range(0, len(planes), size)]


def strips(parts):
    return jnp.concatenate(parts, axis=0).astype(jnp.float32).astype(jnp.bfloat16)


def codes(bits):
    return [bits[0]] + [bits[1 + 2 * k] + 2 * bits[2 + 2 * k] for k in range(SWEEPS)]


def unstrips(ref, height):
    parts = [
        ref[k * height : (k + 1) * height, :].astype(jnp.float32).astype(jnp.int32)
        for k in range(1 + SWEEPS)
    ]
    bits = [parts[0]]
    for code in parts[1:]:
        bits += [code & 1, code >> 1]
    return bits


def spread(word):
    for shift in (4, 8, 16, 32, 64):
        word = word | pltpu.roll(word, shift, 1)
    return word


def sweeps_of(words):
    spins = words[0]
    width = spins.shape[1]
    row = lax.broadcasted_iota(jnp.int32, spins.shape, 0)
    parity = (row + lax.broadcasted_iota(jnp.int32, spins.shape, 1)) & 1
    for k in range(SWEEPS):
        for colour in range(2):
            up = pltpu.roll(spins, 1, 0)
            up = jnp.where(row == 0, up << 1, up)
            down = pltpu.roll(spins, DEPTH - 1, 0)
            down = jnp.where(row == DEPTH - 1, down >> 1, down)
            a, b = up ^ spins, down ^ spins
            c, d = pltpu.roll(spins, 1, 1) ^ spins, pltpu.roll(spins, width - 1, 1) ^ spins
            either, other = a | b, c | d
            some = either | other
            several = (a & b) | (c & d) | (either & other)
            flips = several | (some & words[1 + 2 * k]) | (words[2 + 2 * k] & ~some)
            spins = jnp.where(parity == colour, spins ^ flips, spins)
    return spins


def weigh(spins, moments, plane):
    up = (spins & (jnp.int32(1) << (plane + 1))) != 0
    size = moments.astype(jnp.float32)
    return jnp.where(up, size, -size).astype(jnp.bfloat16)


def middle_kernel(
    odd_ref,
    bar_ref,
    spins_hbm,
    draws_hbm,
    moments_hbm,
    words_ref,
    last_ref,
    first_ref,
    given_ref,
    kept_ref,
    spins_buf,
    draws_buf,
    edge_spins,
    edge_draws,
    moments_buf,
    final_ref,
    bar_smem,
    sems,
    edge_sems,
):
    rows, columns = spins_hbm.shape
    half = rows // DEPTH // 2
    planes = list(range(half - MIDDLE - 1, half + MIDDLE + 1))
    top = planes[0] * DEPTH
    groups = groups_of(planes, PER_STEP)
    size = PER_STEP * DEPTH
    edges = [
        fetch(s, spins_hbm, draws_hbm, edge_spins, edge_draws, edge_sems, row, 8 * s, 8)
        for s, row in enumerate((rows - 8, 0))
    ]
    copies = [
        fetch(
            g,
            spins_hbm,
            draws_hbm,
            spins_buf,
            draws_buf,
            sems,
            top + g * size,
            g * size,
            len(group) * DEPTH,
        )
        for g, group in enumerate(groups)
    ]
    weights = pltpu.make_async_copy(
        moments_hbm.at[pl.ds((half - MIDDLE) * DEPTH, 2 * MIDDLE * DEPTH)],
        moments_buf,
        edge_sems.at[2, 0],
    )
    bars = pltpu.make_async_copy(bar_ref, bar_smem, edge_sems.at[2, 1])
    for copy in [bars] + sum(edges + copies, []) + [weights]:
        copy.start()
    bars.wait()
    bar_ref = bar_smem
    for s, ref in enumerate((last_ref, first_ref)):
        for copy in edges[s]:
            copy.wait()
        parts = [edge_spins[8 * s : 8 * s + 8, :]]
        for k in range(SWEEPS):
            draw = edge_draws[k, 8 * s : 8 * s + 8, :]
            one = (draw < bar_ref[0]).astype(jnp.int32)
            parts.append(one + 2 * (draw < bar_ref[1]).astype(jnp.int32))
        ref[...] = strips(parts + [jnp.zeros_like(parts[0])])
    for g, group in enumerate(groups):
        for copy in copies[g]:
            copy.wait()
        pack(bar_ref, words_ref, spins_buf, draws_buf, group, g * size, g == 0)
    inner = slice(LANES, columns - LANES)
    final_ref[:, inner] = sweeps_of([words_ref[w, :, inner] for w in range(WORDS)])
    weights.wait()
    for ref, lower in ((given_ref, 1 - odd_ref[0]), (kept_ref, odd_ref[0])):
        for i in range(MIDDLE):
            plane = half - MIDDLE + MIDDLE * lower + i
            at = pl.ds(pl.multiple_of((MIDDLE * lower + i) * DEPTH, DEPTH), DEPTH)
            for t in range(ref.shape[0]):
                lanes = pl.ds((t + 1) * TILE, TILE)
                ref[t, i * DEPTH : (i + 1) * DEPTH, :] = weigh(
                    final_ref[:, lanes], moments_buf[at, lanes], plane
                )


def outer_kernel(
    bar_ref,
    spins_hbm,
    draws_hbm,
    middle_ref,
    words_ref,
    spins_buf,
    draws_buf,
    bar_smem,
    sems,
    bar_sem,
):
    bars = pltpu.make_async_copy(bar_ref, bar_smem, bar_sem)
    bars.start()
    planes = spins_hbm.shape[0] // DEPTH
    side = planes // 2 - MIDDLE - 1
    outer = list(range(side)) + list(range(planes - side, planes))
    copies = []
    for g, plane in enumerate(outer):
        copies.append(
            fetch(
                g,
                spins_hbm,
                draws_hbm,
                spins_buf,
                draws_buf,
                sems,
                plane * DEPTH,
                g * DEPTH,
                DEPTH,
            )
        )
        for copy in copies[-1]:
            copy.start()
    words_ref[...] = middle_ref[...]
    bars.wait()
    bar_ref = bar_smem
    for g in range(0, len(outer), PER_STEP):
        group = outer[g : g + PER_STEP]
        for copy in sum(copies[g : g + PER_STEP], []):
            copy.wait()
        pack(bar_ref, words_ref, spins_buf, draws_buf, group, g * DEPTH, False)


def inner_kernel(
    odd_ref,
    words_ref,
    above_ref,
    below_ref,
    moments_hbm,
    spins_ref,
    sides_ref,
    right_ref,
    left_ref,
    given_ref,
    kept_ref,
    joined_ref,
    moments_buf,
    sems,
):
    rows, columns = moments_hbm.shape
    planes = rows // DEPTH
    side = planes // 2 - MIDDLE
    weights = [
        pltpu.make_async_copy(
            moments_hbm.at[pl.ds(row, side * DEPTH)], moments_buf.at[s], sems.at[s]
        )
        for s, row in enumerate((0, rows - side * DEPTH))
    ]
    for copy in weights:
        copy.start()
    above, below = unstrips(above_ref, 8), unstrips(below_ref, 8)
    joined_ref[...] = words_ref[...]
    for w in range(WORDS):
        joined_ref[w, DEPTH - 8 :, :] = words_ref[w, DEPTH - 8 :, :] | above[w]
        joined_ref[w, :8, :] = words_ref[w, :8, :] | (below[w] << (planes + 1))
    lane = lax.broadcasted_iota(jnp.int32, (DEPTH, LANES), 1)
    for ref, at, held in (
        (right_ref, columns - LANES, lane >= LANES - 4),
        (left_ref, 0, lane < 4),
    ):
        bits = []
        for w in range(WORDS):
            edge = jnp.where(held, joined_ref[w, :, at : at + LANES], 0)
            bits.append((spread(edge) >> (lane // 4)) & 1)
        ref[...] = strips(codes(bits))
    reach = TILE + LANES
    sides_ref[:, :, :reach] = joined_ref[:, :, :reach]
    sides_ref[:, :, reach:] = joined_ref[:, :, columns - reach :]
    inner = slice(LANES, columns - LANES)
    spins_ref[:, :LANES] = jnp.zeros((DEPTH, LANES), jnp.int32)
    spins_ref[:, columns - LANES :] = jnp.zeros((DEPTH, LANES), jnp.int32)
    spins_ref[:, inner] = sweeps_of([joined_ref[w, :, inner] for w in range(WORDS)])
    for copy in weights:
        copy.wait()
    for ref, lower in ((given_ref, 1 - odd_ref[0]), (kept_ref, odd_ref[0])):
        for i in range(side):
            plane = (planes - side) * lower + i
            for t in range(ref.shape[0]):
                lanes = pl.ds((t + 1) * TILE, TILE)
                ref[t, i * DEPTH : (i + 1) * DEPTH, :] = weigh(
                    spins_ref[:, lanes],
                    moments_buf[lower, i * DEPTH : (i + 1) * DEPTH, lanes],
                    plane,
                )


def side_kernel(
    odd_ref,
    sides_ref,
    before_ref,
    after_ref,
    moments_hbm,
    spins_ref,
    given_ref,
    kept_ref,
    moments_buf,
    final_ref,
    sems,
):
    rows, columns = moments_hbm.shape
    half = rows // DEPTH // 2
    weights = [
        pltpu.make_async_copy(
            moments_hbm.at[:, pl.ds(at, TILE)], moments_buf.at[s], sems.at[s]
        )
        for s, at in enumerate((0, columns - TILE))
    ]
    for copy in weights:
        copy.start()
    lane = lax.broadcasted_iota(jnp.int32, (DEPTH, LANES), 1)
    before, after = unstrips(before_ref, DEPTH), unstrips(after_ref, DEPTH)
    words = [
        jnp.concatenate(
            [spread(before[w] << (lane // 4)), sides_ref[w], spread(after[w] << (lane // 4))],
            axis=1,
        )
        for w in range(WORDS)
    ]
    updated = sweeps_of(words)
    width = updated.shape[1]
    final_ref[0] = updated[:, LANES : LANES + TILE]
    final_ref[1] = updated[:, width - LANES - TILE : width - LANES]
    spins_ref[...] = final_ref[...]
    for copy in weights:
        copy.wait()
    for ref, lower in ((given_ref, 1 - odd_ref[0]), (kept_ref, odd_ref[0])):
        for i in range(half):
            plane = i + lower * (half + MIDDLE if i < half - MIDDLE else MIDDLE)
            at = pl.ds(pl.multiple_of(plane * DEPTH, DEPTH), DEPTH)
            for s in range(2):
                ref[s, i * DEPTH : (i + 1) * DEPTH, :] = weigh(
                    final_ref[s], moments_buf[s, at, :], plane
                )


def spell_kernel(spins_ref, sides_ref, out_ref):
    columns = out_ref.shape[1]
    first = pl.program_id(0) * PER_STEP + 1
    for plane in range(PER_STEP):
        bit = jnp.int32(1) << (first + plane)
        rows = pl.ds(plane * DEPTH, DEPTH)
        for left in range(0, columns, TILE):
            if left == 0:
                word = sides_ref[0]
            elif left == columns - TILE:
                word = sides_ref[1]
            else:
                word = spins_ref[:, left : left + TILE]
            out_ref[rows, left : left + TILE] = jnp.where((word & bit) != 0, 1.0, -1.0)


def gram(left, right):
    return lax.dot_general(
        left, right, (((0,), (0,)), ((), ())), preferred_element_type=jnp.float32
    )


def stack(refs, first, last):
    return jnp.concatenate(
        [ref[first:last].reshape((last - first) * ref.shape[1], TILE) for ref in refs], axis=0
    )


def fold(sums_ref):
    width = R + LANES
    value = sums_ref[:LANES, :width] + sums_ref[LANES:, LANES : LANES + width]
    height = LANES // 2
    while height >= 8:
        value = value[:height] + pltpu.roll(value[height:], width - height, 1)
        height //= 2
    return value


def own_kernel(*refs):
    parts, (out_ref, sums_ref, full_ref, sems) = refs[:-4], refs[-4:]
    copies = []
    for h in range(2):
        low, high, ends = parts[3 * h : 3 * h + 3]
        split = low.shape[1]
        full = full_ref.at[h]
        tiles = full_ref.shape[1]
        for source, target in (
            (low, full.at[pl.ds(1, tiles - 2), pl.ds(0, split)]),
            (high, full.at[pl.ds(1, tiles - 2), pl.ds(split, high.shape[1])]),
            (ends.at[0], full.at[0]),
            (ends.at[1], full.at[tiles - 1]),
        ):
            copies.append(pltpu.make_async_copy(source, target, sems.at[len(copies)]))
            copies[-1].start()
    for copy in copies:
        copy.wait()
    for n in range(tiles):
        sums_ref[:, n * TILE : (n + 1) * TILE] = sum(
            gram(stack([full_ref.at[h]], 0, tiles - n), stack([full_ref.at[h]], n, tiles))
            for h in range(2)
        )
    sums_ref[:, tiles * TILE :] = jnp.zeros((TILE, TILE), jnp.float32)
    out_ref[...] = fold(sums_ref)


def by_side(odd_ref, own, mid, far, run):
    @pl.when(odd_ref[0] == 0)
    def _():
        run(((own, mid), (mid, far)))

    @pl.when(odd_ref[0] == 1)
    def _():
        run(((far, mid), (mid, own)))


def early_kernel(odd_ref, *refs):
    (base_ref, out_ref, sums_ref) = refs[-3:]
    tiles = refs[0].shape[0]
    sums_ref[:, : 3 * TILE] = jnp.zeros((TILE, 3 * TILE), jnp.float32)

    def run(pairs):
        for n in range(1, tiles + 1):
            sums_ref[:, (n + 2) * TILE : (n + 3) * TILE] = sum(
                gram(stack(left, tiles - n, tiles), stack(right, 0, n)) for left, right in pairs
            )

    by_side(odd_ref, refs[0:2], refs[2:4], refs[4:6], run)
    out_ref[...] = fold(sums_ref) + base_ref[...]


def late_kernel(odd_ref, *refs):
    (base_ref, out_ref, sums_ref) = refs[-3:]
    tiles = refs[0].shape[0] + 2
    sums_ref[:, :TILE] = jnp.zeros((TILE, TILE), jnp.float32)

    def tile(block, t):
        low, high, ends = block
        if t in (0, tiles - 1):
            return ends[min(t, 1)]
        return stack([low, high], t - 1, t)

    def run(pairs):
        for n in range(1, tiles + 1):
            places = [(tiles - 1, n - 1)] + ([(tiles - n, 0)] if n > 1 else [])
            sums_ref[:, n * TILE : (n + 1) * TILE] = sum(
                gram(
                    jnp.concatenate([tile(left, t) for t, _ in places], axis=0),
                    jnp.concatenate([tile(right, q) for _, q in places], axis=0),
                )
                for left, right in pairs
            )

    by_side(odd_ref, refs[0:3], refs[3:6], refs[6:9], run)
    value = fold(sums_ref) + base_ref[...]
    for height in (4, 2, 1):
        value = value + pltpu.roll(pltpu.roll(value, value.shape[1] - height, 1), 8 - height, 0)
    share = out_ref.shape[2]
    for d in range(out_ref.shape[0]):
        out_ref[d] = value[:1, d * share : (d + 1) * share]


def on_device(spins_up, uniforms, moments, accept_bar):
    rows, columns = spins_up.shape
    planes, tiles = rows // DEPTH, columns // TILE
    half_rows, half = rows // 2, planes // 2
    row_devices, col_devices = lax.axis_size("row"), lax.axis_size("col")
    devices = row_devices * col_devices
    assert columns == R and col_devices % 2 == 0 and planes % 2 == 0 and planes + 2 <= 26
    vmem = pl.BlockSpec(memory_space=pltpu.VMEM)
    smem = pl.BlockSpec(memory_space=pltpu.SMEM)
    anywhere = pl.BlockSpec(memory_space=pltpu.HBM)
    strip = jax.ShapeDtypeStruct((8 * (2 + SWEEPS), columns), jnp.bfloat16)
    edge = jax.ShapeDtypeStruct((DEPTH * (1 + SWEEPS), LANES), jnp.bfloat16)
    words_shape = jax.ShapeDtypeStruct((WORDS, DEPTH, columns), jnp.int32)
    dma = pltpu.SemaphoreType.DMA
    odd = (lax.axis_index("col") % 2).reshape(1)
    moments = pltpu.with_memory_space_constraint(moments, pltpu.HBM)
    accept_bar = pltpu.with_memory_space_constraint(accept_bar, pltpu.HBM)

    def message(count, height):
        return jax.ShapeDtypeStruct((count, height, TILE), jnp.bfloat16)

    def ring(size, step):
        return [(i, (i + step) % size) for i in range(size)]

    def exchange(given, kept):
        beside = [(i, i ^ 1) for i in range(col_devices)]
        beyond = [(i, (i - 2 + 4 * (i % 2)) % col_devices) for i in range(col_devices)]
        return lax.ppermute(given, "col", beside), lax.ppermute(kept, "col", beyond)

    def call(kernel, specs, shapes, scratch, flops, moved, *operands):
        return pl.pallas_call(
            kernel,
            in_specs=specs,
            out_specs=jax.tree.map(lambda _: vmem, shapes),
            out_shape=shapes,
            scratch_shapes=scratch,
            compiler_params=params(),
            cost_estimate=pl.CostEstimate(flops=flops, bytes_accessed=moved, transcendentals=0),
        )(*operands)

    packed = (2 * MIDDLE + 2) * DEPTH
    middle = message(tiles - 2, MIDDLE * DEPTH)
    words, last, leading, given, kept = call(
        middle_kernel,
        [smem, anywhere, anywhere, anywhere, anywhere],
        [words_shape, strip, strip, middle, middle],
        [
            pltpu.VMEM((packed, columns), jnp.int32),
            pltpu.VMEM((SWEEPS, packed, columns), jnp.float32),
            pltpu.VMEM((16, columns), jnp.int32),
            pltpu.VMEM((SWEEPS, 16, columns), jnp.float32),
            pltpu.VMEM((2 * MIDDLE * DEPTH, columns), jnp.bfloat16),
            pltpu.VMEM((DEPTH, columns), jnp.int32),
            pltpu.SMEM((2,), jnp.float32),
            dma((pl.cdiv(2 * MIDDLE + 2, PER_STEP), 1 + SWEEPS)),
            dma((3, 1 + SWEEPS)),
        ],
        40 * packed * columns,
        4 * (1 + SWEEPS) * packed * columns,
        odd,
        accept_bar,
        spins_up,
        uniforms,
        moments,
    )
    own = [given, kept]
    got = [*exchange(given, kept)]
    above = lax.ppermute(last, "row", ring(row_devices, 1))
    below = lax.ppermute(leading, "row", ring(row_devices, -1))

    remaining = rows - packed
    words = call(
        outer_kernel,
        [anywhere, anywhere, anywhere, vmem],
        words_shape,
        [
            pltpu.VMEM((remaining, columns), jnp.int32),
            pltpu.VMEM((SWEEPS, remaining, columns), jnp.float32),
            pltpu.SMEM((2,), jnp.float32),
            dma((remaining // DEPTH, 1 + SWEEPS)),
            dma(()),
        ],
        40 * remaining * columns,
        4 * (1 + SWEEPS) * remaining * columns,
        accept_bar,
        spins_up,
        uniforms,
        words,
    )
    side = half - MIDDLE
    low = message(tiles - 2, side * DEPTH)
    reach = 2 * (TILE + LANES)
    spins, sides, right, left, given, kept = call(
        inner_kernel,
        [smem, vmem, vmem, vmem, anywhere],
        [
            jax.ShapeDtypeStruct((DEPTH, columns), jnp.int32),
            jax.ShapeDtypeStruct((WORDS, DEPTH, reach), jnp.int32),
            edge,
            edge,
            low,
            low,
        ],
        [
            pltpu.VMEM(words_shape.shape, jnp.int32),
            pltpu.VMEM((2, side * DEPTH, columns), jnp.bfloat16),
            dma((2,)),
        ],
        40 * rows * columns,
        4 * rows * columns,
        odd,
        words,
        above,
        below,
        moments,
    )
    own = [given, own[0], kept, own[1]]
    mid, far = exchange(given, kept)
    got = [mid, got[0], far, got[1]]
    before = lax.ppermute(right, "col", ring(col_devices, 1))
    after = lax.ppermute(left, "col", ring(col_devices, -1))
    ends = message(2, half_rows)
    side_spins, given, kept = call(
        side_kernel,
        [smem, vmem, vmem, vmem, anywhere],
        [jax.ShapeDtypeStruct((2, DEPTH, TILE), jnp.int32), ends, ends],
        [
            pltpu.VMEM((2, rows, TILE), jnp.bfloat16),
            pltpu.VMEM((2, DEPTH, TILE), jnp.int32),
            dma((2,)),
        ],
        10 * rows * columns,
        rows * columns,
        odd,
        sides,
        before,
        after,
        moments,
    )
    own = [own[0], own[1], given, own[2], own[3], kept]
    mid, far = exchange(given, kept)

    spins_out = pl.pallas_call(
        spell_kernel,
        grid=(rows // (PER_STEP * DEPTH),),
        in_specs=[
            pl.BlockSpec((DEPTH, columns), lambda i: (0, 0)),
            pl.BlockSpec((2, DEPTH, TILE), lambda i: (0, 0, 0)),
        ],
        out_specs=pl.BlockSpec((PER_STEP * DEPTH, columns), lambda i: (i, 0)),
        out_shape=jax.ShapeDtypeStruct((rows, columns), jnp.float32),
        compiler_params=params(),
        cost_estimate=pl.CostEstimate(
            flops=rows * columns, bytes_accessed=4 * rows * columns, transcendentals=0
        ),
        name="spell",
    )(spins, side_spins)
    sums = pltpu.VMEM((TILE, R + TILE), jnp.float32)
    folded = jax.ShapeDtypeStruct((8, R + LANES), jnp.float32)
    work = rows * columns * columns
    base = call(
        own_kernel,
        [vmem] * 6,
        folded,
        [sums, pltpu.VMEM((2, tiles, half_rows, TILE), jnp.bfloat16), dma((8,))],
        work,
        2 * rows * columns,
        *own,
    )
    base = call(
        early_kernel,
        [smem] + [vmem] * 7,
        folded,
        [sums],
        work // 2,
        2 * rows * columns,
        odd,
        own[3],
        own[4],
        *got,
        base,
    )
    partial_sums = call(
        late_kernel,
        [smem] + [vmem] * 10,
        jax.ShapeDtypeStruct((devices, 1, R // devices), jnp.float32),
        [sums],
        work // 2,
        2 * rows * columns,
        odd,
        own[3],
        own[4],
        own[5],
        got[0],
        got[1],
        mid,
        got[2],
        got[3],
        far,
        base,
    )
    normaliser = 1.0 / math.sqrt(rows * row_devices * columns * col_devices)
    shares = lax.all_to_all(partial_sums, ("row", "col"), 0, 0, tiled=True)
    return spins_out, jnp.sum(shares, axis=(0, 1)) * normaliser


def solution(mesh):
    placed = (P("row", "col"), P(None, "row", "col"), P("row", "col"), P())
    return jax.shard_map(
        on_device,
        mesh=mesh,
        in_specs=placed,
        out_specs=(P("row", "col"), P(("row", "col"))),
        check_vma=False,
    )
```

```python
import functools
import math

import jax
import jax.numpy as jnp
from jax import lax
from jax.experimental import pallas as pl
from jax.experimental.pallas import tpu as pltpu
from jax.sharding import PartitionSpec as P

R = 2048
SWEEPS = 2
DEPTH = 32
LANES = 128
TILE = 256
PER_STEP = 2
MIDDLE = 6
WORDS = 1 + 2 * SWEEPS


def params(**more):
    return pltpu.CompilerParams(vmem_limit_bytes=48 << 20, **more)


def fetch(step, spins_hbm, draws_hbm, spins_buf, draws_buf, sems, row, at, count):
    copies = [
        pltpu.make_async_copy(
            spins_hbm.at[pl.ds(row, count)], spins_buf.at[pl.ds(at, count)], sems.at[step, 0]
        )
    ]
    for k in range(SWEEPS):
        copies.append(
            pltpu.make_async_copy(
                draws_hbm.at[k, pl.ds(row, count)],
                draws_buf.at[k, pl.ds(at, count)],
                sems.at[step, 1 + k],
            )
        )
    return copies


def pack(bar_ref, words_ref, spins_buf, draws_buf, planes, at, fresh):
    columns = words_ref.shape[2]
    for left in range(0, columns, TILE):
        lanes = pl.ds(left, TILE)
        if fresh:
            words = [jnp.zeros((DEPTH, TILE), jnp.int32)] * WORDS
        else:
            words = [words_ref[w, :, lanes] for w in range(WORDS)]
        for i, plane in enumerate(planes):
            bit = 1 << (plane + 1)
            rows = pl.ds(at + i * DEPTH, DEPTH)
            words[0] = words[0] | (spins_buf[rows, lanes] << (plane + 1))
            for k in range(SWEEPS):
                draw = draws_buf[k, rows, lanes]
                for c in range(2):
                    word = words[1 + 2 * k + c]
                    words[1 + 2 * k + c] = jnp.where(draw < bar_ref[c], word | bit, word)
        for w, word in enumerate(words):
            words_ref[w, :, lanes] = word


def groups_of(planes, size):
    return [planes[i : i + size] for i in range(0, len(planes), size)]


def strips(parts):
    return jnp.concatenate(parts, axis=0).astype(jnp.float32).astype(jnp.bfloat16)


def codes(bits):
    return [bits[0]] + [bits[1 + 2 * k] + 2 * bits[2 + 2 * k] for k in range(SWEEPS)]


def unstrips(ref, height):
    parts = [
        ref[k * height : (k + 1) * height, :].astype(jnp.float32).astype(jnp.int32)
        for k in range(1 + SWEEPS)
    ]
    bits = [parts[0]]
    for code in parts[1:]:
        bits += [code & 1, code >> 1]
    return bits


def spread(word):
    for shift in (4, 8, 16, 32, 64):
        word = word | pltpu.roll(word, shift, 1)
    return word


def sweeps_of(words):
    spins = words[0]
    width = spins.shape[1]
    row = lax.broadcasted_iota(jnp.int32, spins.shape, 0)
    parity = (row + lax.broadcasted_iota(jnp.int32, spins.shape, 1)) & 1
    for k in range(SWEEPS):
        for colour in range(2):
            up = pltpu.roll(spins, 1, 0)
            up = jnp.where(row == 0, up << 1, up)
            down = pltpu.roll(spins, DEPTH - 1, 0)
            down = jnp.where(row == DEPTH - 1, down >> 1, down)
            a, b = up ^ spins, down ^ spins
            c, d = pltpu.roll(spins, 1, 1) ^ spins, pltpu.roll(spins, width - 1, 1) ^ spins
            either, other = a | b, c | d
            some = either | other
            several = (a & b) | (c & d) | (either & other)
            flips = several | (some & words[1 + 2 * k]) | (words[2 + 2 * k] & ~some)
            spins = jnp.where(parity == colour, spins ^ flips, spins)
    return spins


def weigh(spins, moments, plane):
    up = (spins & (jnp.int32(1) << (plane + 1))) != 0
    return jnp.where(up, 1.0, -1.0).astype(jnp.bfloat16) * moments


def middle_kernel(
    odd_ref,
    bar_ref,
    spins_hbm,
    draws_hbm,
    moments_hbm,
    words_ref,
    last_ref,
    first_ref,
    given_ref,
    kept_ref,
    spins_buf,
    draws_buf,
    edge_spins,
    edge_draws,
    moments_buf,
    final_ref,
    bar_smem,
    sems,
    edge_sems,
):
    rows, columns = spins_hbm.shape
    half = rows // DEPTH // 2
    planes = list(range(half - MIDDLE - 1, half + MIDDLE + 1))
    top = planes[0] * DEPTH
    groups = groups_of(planes, PER_STEP)
    size = PER_STEP * DEPTH
    edges = [
        fetch(s, spins_hbm, draws_hbm, edge_spins, edge_draws, edge_sems, row, 8 * s, 8)
        for s, row in enumerate((rows - 8, 0))
    ]
    copies = [
        fetch(
            g,
            spins_hbm,
            draws_hbm,
            spins_buf,
            draws_buf,
            sems,
            top + g * size,
            g * size,
            len(group) * DEPTH,
        )
        for g, group in enumerate(groups)
    ]
    weights = pltpu.make_async_copy(
        moments_hbm.at[pl.ds((half - MIDDLE) * DEPTH, 2 * MIDDLE * DEPTH)],
        moments_buf,
        edge_sems.at[2, 0],
    )
    bars = pltpu.make_async_copy(bar_ref, bar_smem, edge_sems.at[2, 1])
    for copy in [bars] + sum(edges + copies, []) + [weights]:
        copy.start()
    bars.wait()
    bar_ref = bar_smem
    for s, ref in enumerate((last_ref, first_ref)):
        for copy in edges[s]:
            copy.wait()
        parts = [edge_spins[8 * s : 8 * s + 8, :]]
        for k in range(SWEEPS):
            draw = edge_draws[k, 8 * s : 8 * s + 8, :]
            one = (draw < bar_ref[0]).astype(jnp.int32)
            parts.append(one + 2 * (draw < bar_ref[1]).astype(jnp.int32))
        ref[...] = strips(parts + [jnp.zeros_like(parts[0])])
    for g, group in enumerate(groups):
        for copy in copies[g]:
            copy.wait()
        pack(bar_ref, words_ref, spins_buf, draws_buf, group, g * size, g == 0)
    inner = slice(LANES, columns - LANES)
    final_ref[:, inner] = sweeps_of([words_ref[w, :, inner] for w in range(WORDS)])
    weights.wait()
    for ref, lower in ((given_ref, 1 - odd_ref[0]), (kept_ref, odd_ref[0])):
        for i in range(MIDDLE):
            plane = half - MIDDLE + MIDDLE * lower + i
            at = pl.ds(pl.multiple_of((MIDDLE * lower + i) * DEPTH, DEPTH), DEPTH)
            for t in range(ref.shape[0]):
                lanes = pl.ds((t + 1) * TILE, TILE)
                ref[t, i * DEPTH : (i + 1) * DEPTH, :] = weigh(
                    final_ref[:, lanes], moments_buf[at, lanes], plane
                )


def outer_kernel(
    bar_ref,
    spins_hbm,
    draws_hbm,
    middle_ref,
    words_ref,
    spins_buf,
    draws_buf,
    bar_smem,
    sems,
    bar_sem,
):
    bars = pltpu.make_async_copy(bar_ref, bar_smem, bar_sem)
    bars.start()
    planes = spins_hbm.shape[0] // DEPTH
    side = planes // 2 - MIDDLE - 1
    outer = list(range(side)) + list(range(planes - side, planes))
    copies = []
    for g, plane in enumerate(outer):
        copies.append(
            fetch(
                g,
                spins_hbm,
                draws_hbm,
                spins_buf,
                draws_buf,
                sems,
                plane * DEPTH,
                g * DEPTH,
                DEPTH,
            )
        )
        for copy in copies[-1]:
            copy.start()
    words_ref[...] = middle_ref[...]
    bars.wait()
    bar_ref = bar_smem
    for g in range(0, len(outer), PER_STEP):
        group = outer[g : g + PER_STEP]
        for copy in sum(copies[g : g + PER_STEP], []):
            copy.wait()
        pack(bar_ref, words_ref, spins_buf, draws_buf, group, g * DEPTH, False)


def inner_kernel(
    odd_ref,
    words_ref,
    above_ref,
    below_ref,
    moments_hbm,
    spins_ref,
    sides_ref,
    right_ref,
    left_ref,
    given_ref,
    kept_ref,
    joined_ref,
    moments_buf,
    sems,
):
    rows, columns = moments_hbm.shape
    planes = rows // DEPTH
    side = planes // 2 - MIDDLE
    weights = [
        pltpu.make_async_copy(
            moments_hbm.at[pl.ds(row, side * DEPTH)], moments_buf.at[s], sems.at[s]
        )
        for s, row in enumerate((0, rows - side * DEPTH))
    ]
    for copy in weights:
        copy.start()
    above, below = unstrips(above_ref, 8), unstrips(below_ref, 8)
    joined_ref[...] = words_ref[...]
    for w in range(WORDS):
        joined_ref[w, DEPTH - 8 :, :] = words_ref[w, DEPTH - 8 :, :] | above[w]
        joined_ref[w, :8, :] = words_ref[w, :8, :] | (below[w] << (planes + 1))
    lane = lax.broadcasted_iota(jnp.int32, (DEPTH, LANES), 1)
    for ref, at, held in (
        (right_ref, columns - LANES, lane >= LANES - 4),
        (left_ref, 0, lane < 4),
    ):
        bits = []
        for w in range(WORDS):
            edge = jnp.where(held, joined_ref[w, :, at : at + LANES], 0)
            bits.append((spread(edge) >> (lane // 4)) & 1)
        ref[...] = strips(codes(bits))
    reach = TILE + LANES
    sides_ref[:, :, :reach] = joined_ref[:, :, :reach]
    sides_ref[:, :, reach:] = joined_ref[:, :, columns - reach :]
    inner = slice(LANES, columns - LANES)
    spins_ref[:, :LANES] = jnp.zeros((DEPTH, LANES), jnp.int32)
    spins_ref[:, columns - LANES :] = jnp.zeros((DEPTH, LANES), jnp.int32)
    spins_ref[:, inner] = sweeps_of([joined_ref[w, :, inner] for w in range(WORDS)])
    for copy in weights:
        copy.wait()
    for ref, lower in ((given_ref, 1 - odd_ref[0]), (kept_ref, odd_ref[0])):
        for i in range(side):
            plane = (planes - side) * lower + i
            for t in range(ref.shape[0]):
                lanes = pl.ds((t + 1) * TILE, TILE)
                ref[t, i * DEPTH : (i + 1) * DEPTH, :] = weigh(
                    spins_ref[:, lanes],
                    moments_buf[lower, i * DEPTH : (i + 1) * DEPTH, lanes],
                    plane,
                )


def side_kernel(
    odd_ref,
    sides_ref,
    before_ref,
    after_ref,
    moments_hbm,
    spins_ref,
    given_ref,
    kept_ref,
    moments_buf,
    final_ref,
    sems,
):
    rows, columns = moments_hbm.shape
    half = rows // DEPTH // 2
    weights = [
        pltpu.make_async_copy(
            moments_hbm.at[:, pl.ds(at, TILE)], moments_buf.at[s], sems.at[s]
        )
        for s, at in enumerate((0, columns - TILE))
    ]
    for copy in weights:
        copy.start()
    lane = lax.broadcasted_iota(jnp.int32, (DEPTH, LANES), 1)
    before, after = unstrips(before_ref, DEPTH), unstrips(after_ref, DEPTH)
    words = [
        jnp.concatenate(
            [spread(before[w] << (lane // 4)), sides_ref[w], spread(after[w] << (lane // 4))],
            axis=1,
        )
        for w in range(WORDS)
    ]
    updated = sweeps_of(words)
    width = updated.shape[1]
    final_ref[0] = updated[:, LANES : LANES + TILE]
    final_ref[1] = updated[:, width - LANES - TILE : width - LANES]
    spins_ref[...] = final_ref[...]
    for copy in weights:
        copy.wait()
    for ref, lower in ((given_ref, 1 - odd_ref[0]), (kept_ref, odd_ref[0])):
        for i in range(half):
            plane = i + lower * (half + MIDDLE if i < half - MIDDLE else MIDDLE)
            at = pl.ds(pl.multiple_of(plane * DEPTH, DEPTH), DEPTH)
            for s in range(2):
                ref[s, i * DEPTH : (i + 1) * DEPTH, :] = weigh(
                    final_ref[s], moments_buf[s, at, :], plane
                )


def spell_kernel(spins_ref, sides_ref, out_ref):
    columns = out_ref.shape[1]
    first = pl.program_id(0) * PER_STEP + 1
    for plane in range(PER_STEP):
        bit = jnp.int32(1) << (first + plane)
        rows = pl.ds(plane * DEPTH, DEPTH)
        for left in range(0, columns, TILE):
            if left == 0:
                word = sides_ref[0]
            elif left == columns - TILE:
                word = sides_ref[1]
            else:
                word = spins_ref[:, left : left + TILE]
            out_ref[rows, left : left + TILE] = jnp.where((word & bit) != 0, 1.0, -1.0)


def gram(left, right):
    return lax.dot_general(
        left, right, (((0,), (0,)), ((), ())), preferred_element_type=jnp.float32
    )


def stack(refs, first, last):
    return jnp.concatenate(
        [ref[first:last].reshape((last - first) * ref.shape[1], TILE) for ref in refs], axis=0
    )


def fold(sums_ref):
    width = R + LANES
    value = sums_ref[:LANES, :width] + sums_ref[LANES:, LANES : LANES + width]
    height = LANES // 2
    while height >= 8:
        value = value[:height] + pltpu.roll(value[height:], width - height, 1)
        height //= 2
    return value


def tile(block, t):
    low, high, ends = block
    last = low.shape[0] + 1
    if t in (0, last):
        return ends[min(t, 1)]
    return stack([low, high], t - 1, t)


def tiles_of(block, places):
    return jnp.concatenate([tile(block, t) for t in places], axis=0)


def own_kernel(*refs):
    parts, (out_ref, sums_ref) = refs[:-2], refs[-2:]
    blocks = (parts[:3], parts[3:])
    tiles = parts[0].shape[0] + 2
    for n in range(tiles):
        sums_ref[:, n * TILE : (n + 1) * TILE] = sum(
            gram(tiles_of(block, range(tiles - n)), tiles_of(block, range(n, tiles)))
            for block in blocks
        )
    sums_ref[:, tiles * TILE :] = jnp.zeros((TILE, TILE), jnp.float32)
    out_ref[...] = fold(sums_ref)


def by_side(odd_ref, own, mid, far, run):
    @pl.when(odd_ref[0] == 0)
    def _():
        run(((own, mid), (mid, far)))

    @pl.when(odd_ref[0] == 1)
    def _():
        run(((far, mid), (mid, own)))


def early_kernel(odd_ref, *refs):
    (base_ref, out_ref, sums_ref) = refs[-3:]
    tiles = refs[0].shape[0]
    sums_ref[:, : 3 * TILE] = jnp.zeros((TILE, 3 * TILE), jnp.float32)

    def run(pairs):
        for n in range(1, tiles + 1):
            sums_ref[:, (n + 2) * TILE : (n + 3) * TILE] = sum(
                gram(stack(left, tiles - n, tiles), stack(right, 0, n)) for left, right in pairs
            )

    by_side(odd_ref, refs[0:2], refs[2:4], refs[4:6], run)
    out_ref[...] = fold(sums_ref) + base_ref[...]


def late_kernel(scale, odd_ref, *refs):
    (base_ref, out_ref, sums_ref) = refs[-3:]
    tiles = refs[0].shape[0] + 2
    sums_ref[:, :TILE] = jnp.zeros((TILE, TILE), jnp.float32)

    def run(pairs):
        for n in range(1, tiles + 1):
            places = [(tiles - 1, n - 1)] + ([(tiles - n, 0)] if n > 1 else [])
            sums_ref[:, n * TILE : (n + 1) * TILE] = sum(
                gram(tiles_of(left, [t for t, _ in places]), tiles_of(right, [q for _, q in places]))
                for left, right in pairs
            )

    by_side(odd_ref, refs[0:3], refs[3:6], refs[6:9], run)
    value = fold(sums_ref) + base_ref[...]
    for height in (4, 2, 1):
        value = value + pltpu.roll(pltpu.roll(value, value.shape[1] - height, 1), 8 - height, 0)
    value = value[:1] * scale
    share = out_ref.shape[2]
    for d in range(out_ref.shape[0]):
        out_ref[d] = value[:, d * share : (d + 1) * share]


def on_device(spins_up, uniforms, moments, accept_bar):
    rows, columns = spins_up.shape
    planes, tiles = rows // DEPTH, columns // TILE
    half_rows, half = rows // 2, planes // 2
    row_devices, col_devices = lax.axis_size("row"), lax.axis_size("col")
    devices = row_devices * col_devices
    assert columns == R and col_devices % 2 == 0 and planes % 2 == 0 and planes + 2 <= 26
    vmem = pl.BlockSpec(memory_space=pltpu.VMEM)
    smem = pl.BlockSpec(memory_space=pltpu.SMEM)
    anywhere = pl.BlockSpec(memory_space=pltpu.HBM)
    strip = jax.ShapeDtypeStruct((8 * (2 + SWEEPS), columns), jnp.bfloat16)
    edge = jax.ShapeDtypeStruct((DEPTH * (1 + SWEEPS), LANES), jnp.bfloat16)
    words_shape = jax.ShapeDtypeStruct((WORDS, DEPTH, columns), jnp.int32)
    dma = pltpu.SemaphoreType.DMA
    odd = (lax.axis_index("col") % 2).reshape(1)
    moments = pltpu.with_memory_space_constraint(moments, pltpu.HBM)
    accept_bar = pltpu.with_memory_space_constraint(accept_bar, pltpu.HBM)

    def message(count, height):
        return jax.ShapeDtypeStruct((count, height, TILE), jnp.bfloat16)

    def ring(size, step):
        return [(i, (i + step) % size) for i in range(size)]

    def exchange(given, kept):
        beside = [(i, i ^ 1) for i in range(col_devices)]
        beyond = [(i, (i - 2 + 4 * (i % 2)) % col_devices) for i in range(col_devices)]
        return lax.ppermute(given, "col", beside), lax.ppermute(kept, "col", beyond)

    def call(kernel, specs, shapes, scratch, flops, moved, *operands):
        return pl.pallas_call(
            kernel,
            in_specs=specs,
            out_specs=jax.tree.map(lambda _: vmem, shapes),
            out_shape=shapes,
            scratch_shapes=scratch,
            compiler_params=params(),
            cost_estimate=pl.CostEstimate(flops=flops, bytes_accessed=moved, transcendentals=0),
        )(*operands)

    packed = (2 * MIDDLE + 2) * DEPTH
    middle = message(tiles - 2, MIDDLE * DEPTH)
    words, last, leading, given, kept = call(
        middle_kernel,
        [smem, anywhere, anywhere, anywhere, anywhere],
        [words_shape, strip, strip, middle, middle],
        [
            pltpu.VMEM((packed, columns), jnp.int32),
            pltpu.VMEM((SWEEPS, packed, columns), jnp.float32),
            pltpu.VMEM((16, columns), jnp.int32),
            pltpu.VMEM((SWEEPS, 16, columns), jnp.float32),
            pltpu.VMEM((2 * MIDDLE * DEPTH, columns), jnp.bfloat16),
            pltpu.VMEM((DEPTH, columns), jnp.int32),
            pltpu.SMEM((2,), jnp.float32),
            dma((pl.cdiv(2 * MIDDLE + 2, PER_STEP), 1 + SWEEPS)),
            dma((3, 1 + SWEEPS)),
        ],
        40 * packed * columns,
        4 * (1 + SWEEPS) * packed * columns,
        odd,
        accept_bar,
        spins_up,
        uniforms,
        moments,
    )
    own = [given, kept]
    got = [*exchange(given, kept)]
    above = lax.ppermute(last, "row", ring(row_devices, 1))
    below = lax.ppermute(leading, "row", ring(row_devices, -1))

    remaining = rows - packed
    words = call(
        outer_kernel,
        [anywhere, anywhere, anywhere, vmem],
        words_shape,
        [
            pltpu.VMEM((remaining, columns), jnp.int32),
            pltpu.VMEM((SWEEPS, remaining, columns), jnp.float32),
            pltpu.SMEM((2,), jnp.float32),
            dma((remaining // DEPTH, 1 + SWEEPS)),
            dma(()),
        ],
        40 * remaining * columns,
        4 * (1 + SWEEPS) * remaining * columns,
        accept_bar,
        spins_up,
        uniforms,
        words,
    )
    side = half - MIDDLE
    low = message(tiles - 2, side * DEPTH)
    reach = 2 * (TILE + LANES)
    spins, sides, right, left, given, kept = call(
        inner_kernel,
        [smem, vmem, vmem, vmem, anywhere],
        [
            jax.ShapeDtypeStruct((DEPTH, columns), jnp.int32),
            jax.ShapeDtypeStruct((WORDS, DEPTH, reach), jnp.int32),
            edge,
            edge,
            low,
            low,
        ],
        [
            pltpu.VMEM(words_shape.shape, jnp.int32),
            pltpu.VMEM((2, side * DEPTH, columns), jnp.bfloat16),
            dma((2,)),
        ],
        40 * rows * columns,
        4 * rows * columns,
        odd,
        words,
        above,
        below,
        moments,
    )
    own = [given, own[0], kept, own[1]]
    mid, far = exchange(given, kept)
    got = [mid, got[0], far, got[1]]
    before = lax.ppermute(right, "col", ring(col_devices, 1))
    after = lax.ppermute(left, "col", ring(col_devices, -1))
    ends = message(2, half_rows)
    side_spins, given, kept = call(
        side_kernel,
        [smem, vmem, vmem, vmem, anywhere],
        [jax.ShapeDtypeStruct((2, DEPTH, TILE), jnp.int32), ends, ends],
        [
            pltpu.VMEM((2, rows, TILE), jnp.bfloat16),
            pltpu.VMEM((2, DEPTH, TILE), jnp.int32),
            dma((2,)),
        ],
        10 * rows * columns,
        rows * columns,
        odd,
        sides,
        before,
        after,
        moments,
    )
    own = [own[0], own[1], given, own[2], own[3], kept]
    mid, far = exchange(given, kept)

    spins_out = pl.pallas_call(
        spell_kernel,
        grid=(rows // (PER_STEP * DEPTH),),
        in_specs=[
            pl.BlockSpec((DEPTH, columns), lambda i: (0, 0)),
            pl.BlockSpec((2, DEPTH, TILE), lambda i: (0, 0, 0)),
        ],
        out_specs=pl.BlockSpec((PER_STEP * DEPTH, columns), lambda i: (i, 0)),
        out_shape=jax.ShapeDtypeStruct((rows, columns), jnp.float32),
        compiler_params=params(),
        cost_estimate=pl.CostEstimate(
            flops=rows * columns, bytes_accessed=4 * rows * columns, transcendentals=0
        ),
        name="spell",
    )(spins, side_spins)
    normaliser = 1.0 / math.sqrt(rows * row_devices * columns * col_devices)
    sums = pltpu.VMEM((TILE, R + TILE), jnp.float32)
    folded = jax.ShapeDtypeStruct((8, R + LANES), jnp.float32)
    work = rows * columns * columns
    base = call(own_kernel, [vmem] * 6, folded, [sums], work, 2 * rows * columns, *own)
    base = call(
        early_kernel,
        [smem] + [vmem] * 7,
        folded,
        [sums],
        work // 2,
        2 * rows * columns,
        odd,
        own[3],
        own[4],
        *got,
        base,
    )
    partial_sums = call(
        functools.partial(late_kernel, normaliser),
        [smem] + [vmem] * 10,
        jax.ShapeDtypeStruct((devices, 1, R // devices), jnp.float32),
        [sums],
        work // 2,
        2 * rows * columns,
        odd,
        own[3],
        own[4],
        own[5],
        got[0],
        got[1],
        mid,
        got[2],
        got[3],
        far,
        base,
    )
    shares = lax.all_to_all(partial_sums, ("row", "col"), 0, 0, tiled=True)
    return spins_out, jnp.sum(shares, axis=(0, 1))


def solution(mesh):
    placed = (P("row", "col"), P(None, "row", "col"), P("row", "col"), P())
    return jax.shard_map(
        on_device,
        mesh=mesh,
        in_specs=placed,
        out_specs=(P("row", "col"), P(("row", "col"))),
        check_vma=False,
    )
```

```python
import functools
import math

import jax
import jax.numpy as jnp
from jax import lax
from jax.experimental import pallas as pl
from jax.experimental.pallas import tpu as pltpu
from jax.sharding import PartitionSpec as P

R = 2048
SWEEPS = 2
DEPTH = 32
LANES = 128
TILE = 256
PER_STEP = 2
MIDDLE = 4
WORDS = 1 + 2 * SWEEPS


def params(**more):
    return pltpu.CompilerParams(vmem_limit_bytes=48 << 20, **more)


def fetch(step, spins_hbm, draws_hbm, spins_buf, draws_buf, sems, row, at, count):
    copies = [
        pltpu.make_async_copy(
            spins_hbm.at[pl.ds(row, count)], spins_buf.at[pl.ds(at, count)], sems.at[step, 0]
        )
    ]
    for k in range(SWEEPS):
        copies.append(
            pltpu.make_async_copy(
                draws_hbm.at[k, pl.ds(row, count)],
                draws_buf.at[k, pl.ds(at, count)],
                sems.at[step, 1 + k],
            )
        )
    return copies


def pack(bar_ref, words_ref, spins_buf, draws_buf, planes, at, fresh):
    columns = words_ref.shape[2]
    for left in range(0, columns, TILE):
        lanes = pl.ds(left, TILE)
        if fresh:
            words = [jnp.zeros((DEPTH, TILE), jnp.int32)] * WORDS
        else:
            words = [words_ref[w, :, lanes] for w in range(WORDS)]
        for i, plane in enumerate(planes):
            bit = 1 << (plane + 1)
            rows = pl.ds(at + i * DEPTH, DEPTH)
            words[0] = words[0] | (spins_buf[rows, lanes] << (plane + 1))
            for k in range(SWEEPS):
                draw = draws_buf[k, rows, lanes]
                for c in range(2):
                    word = words[1 + 2 * k + c]
                    words[1 + 2 * k + c] = jnp.where(draw < bar_ref[c], word | bit, word)
        for w, word in enumerate(words):
            words_ref[w, :, lanes] = word


def groups_of(planes, size):
    return [planes[i : i + size] for i in range(0, len(planes), size)]


def strips(parts):
    return jnp.concatenate(parts, axis=0).astype(jnp.float32).astype(jnp.bfloat16)


def codes(bits):
    return [bits[0]] + [bits[1 + 2 * k] + 2 * bits[2 + 2 * k] for k in range(SWEEPS)]


def unstrips(ref, height):
    parts = [
        ref[k * height : (k + 1) * height, :].astype(jnp.float32).astype(jnp.int32)
        for k in range(1 + SWEEPS)
    ]
    bits = [parts[0]]
    for code in parts[1:]:
        bits += [code & 1, code >> 1]
    return bits


def spread(word):
    for shift in (4, 8, 16, 32, 64):
        word = word | pltpu.roll(word, shift, 1)
    return word


def sweeps_of(words):
    spins = words[0]
    width = spins.shape[1]
    row = lax.broadcasted_iota(jnp.int32, spins.shape, 0)
    parity = (row + lax.broadcasted_iota(jnp.int32, spins.shape, 1)) & 1
    for k in range(SWEEPS):
        for colour in range(2):
            up = pltpu.roll(spins, 1, 0)
            up = jnp.where(row == 0, up << 1, up)
            down = pltpu.roll(spins, DEPTH - 1, 0)
            down = jnp.where(row == DEPTH - 1, down >> 1, down)
            a, b = up ^ spins, down ^ spins
            c, d = pltpu.roll(spins, 1, 1) ^ spins, pltpu.roll(spins, width - 1, 1) ^ spins
            either, other = a | b, c | d
            some = either | other
            several = (a & b) | (c & d) | (either & other)
            flips = several | (some & words[1 + 2 * k]) | (words[2 + 2 * k] & ~some)
            spins = jnp.where(parity == colour, spins ^ flips, spins)
    return spins


def weigh(spins, moments, plane):
    up = (spins & (jnp.int32(1) << (plane + 1))) != 0
    return jnp.where(up, 1.0, -1.0).astype(jnp.bfloat16) * moments


def select(odd, when_odd, when_even):
    return jnp.where(odd == 1, when_odd, when_even)


def fill(refs, odd, planes_of, moments_of, spins_of):
    for ref, lower in zip(refs, (1 - odd, odd)):
        for i, plane in enumerate(planes_of(lower)):
            for t in range(ref.shape[0]):
                ref[t, i * DEPTH : (i + 1) * DEPTH, :] = weigh(
                    spins_of(t), moments_of(lower, i, t), plane
                )


def middle_kernel(
    odd_ref,
    bar_hbm,
    spins_hbm,
    draws_hbm,
    moments_hbm,
    words_ref,
    beside_ref,
    across_ref,
    given_ref,
    kept_ref,
    spins_buf,
    draws_buf,
    edge_spins,
    edge_draws,
    moments_buf,
    final_ref,
    bar_ref,
    sems,
    edge_sems,
):
    rows, columns = spins_hbm.shape
    half = rows // DEPTH // 2
    planes = list(range(half - MIDDLE - 1, half + MIDDLE + 1))
    top = planes[0] * DEPTH
    groups = groups_of(planes, PER_STEP)
    size = PER_STEP * DEPTH
    bars = pltpu.make_async_copy(bar_hbm, bar_ref, edge_sems.at[4, 1])
    edges = []
    for e, (at, row) in enumerate(
        (at, row) for at in (0, columns - LANES) for row in (0, rows - top)
    ):
        source = (pl.ds(row, top), pl.ds(at, LANES))
        edges.append(
            pltpu.make_async_copy(spins_hbm.at[source], edge_spins.at[e], edge_sems.at[e, 0])
        )
        for k in range(SWEEPS):
            edges.append(
                pltpu.make_async_copy(
                    draws_hbm.at[(k, *source)], edge_draws.at[k, e], edge_sems.at[e, 1 + k]
                )
            )
    copies = [
        fetch(
            g,
            spins_hbm,
            draws_hbm,
            spins_buf,
            draws_buf,
            sems,
            top + g * size,
            g * size,
            len(group) * DEPTH,
        )
        for g, group in enumerate(groups)
    ]
    weights = pltpu.make_async_copy(
        moments_hbm.at[pl.ds((half - MIDDLE) * DEPTH, 2 * MIDDLE * DEPTH)],
        moments_buf,
        edge_sems.at[4, 0],
    )
    for copy in [bars] + edges + sum(copies, []) + [weights]:
        copy.start()
    bars.wait()
    for copy in edges:
        copy.wait()
    side_words = []
    for e in range(4):
        if e % 2 == 0:
            side_words.append([jnp.zeros((DEPTH, LANES), jnp.int32)] * WORDS)
        words = side_words[-1]
        for i in range(top // DEPTH):
            plane = i + (e % 2) * (rows - top) // DEPTH
            at = pl.ds(i * DEPTH, DEPTH)
            words[0] = words[0] | (edge_spins[e, at, :] << (plane + 1))
            for k in range(SWEEPS):
                draw = edge_draws[k, e, at, :]
                for c in range(2):
                    word = words[1 + 2 * k + c]
                    words[1 + 2 * k + c] = jnp.where(
                        draw < bar_ref[c], word | (1 << (plane + 1)), word
                    )
    for g, group in enumerate(groups):
        for copy in copies[g]:
            copy.wait()
        pack(bar_ref, words_ref, spins_buf, draws_buf, group, g * size, g == 0)
    lane = lax.broadcasted_iota(jnp.int32, (DEPTH, LANES), 1)
    codes_of = []
    for at, held, outer in (
        (0, lane < 4, side_words[0]),
        (columns - LANES, lane >= LANES - 4, side_words[1]),
    ):
        bits = []
        for w in range(WORDS):
            edge = jnp.where(held, words_ref[w, :, at : at + LANES] | outer[w], 0)
            bits.append((spread(edge) >> (lane // 4)) & 1)
        codes_of.append(jnp.concatenate(codes(bits), axis=0).astype(jnp.float32))
    odd = odd_ref[0]
    beside_ref[...] = select(odd, codes_of[0], codes_of[1]).astype(jnp.bfloat16)
    across_ref[...] = select(odd, codes_of[1], codes_of[0]).astype(jnp.bfloat16)
    inner = slice(LANES, columns - LANES)
    final_ref[:, inner] = sweeps_of([words_ref[w, :, inner] for w in range(WORDS)])
    weights.wait()
    fill(
        (given_ref, kept_ref),
        odd,
        lambda lower: [half - MIDDLE + MIDDLE * lower + i for i in range(MIDDLE)],
        lambda lower, i, t: moments_buf[
            pl.ds(pl.multiple_of((MIDDLE * lower + i) * DEPTH, DEPTH), DEPTH),
            pl.ds((t + 1) * TILE, TILE),
        ],
        lambda t: final_ref[:, pl.ds((t + 1) * TILE, TILE)],
    )


def outer_kernel(
    odd_ref,
    bar_hbm,
    spins_hbm,
    draws_hbm,
    moments_hbm,
    middle_ref,
    words_ref,
    given_ref,
    kept_ref,
    spins_buf,
    draws_buf,
    moments_buf,
    final_ref,
    bar_ref,
    sems,
    more_sems,
):
    rows, columns = spins_hbm.shape
    planes = rows // DEPTH
    side = planes // 2 - MIDDLE - 1
    outer = list(range(side)) + list(range(planes - side, planes))
    bars = pltpu.make_async_copy(bar_hbm, bar_ref, more_sems.at[2])
    bars.start()
    copies = []
    for g, plane in enumerate(outer):
        copies.append(
            fetch(
                g,
                spins_hbm,
                draws_hbm,
                spins_buf,
                draws_buf,
                sems,
                plane * DEPTH,
                g * DEPTH,
                DEPTH,
            )
        )
        for copy in copies[-1]:
            copy.start()
    weights = [
        pltpu.make_async_copy(
            moments_hbm.at[pl.ds(row, side * DEPTH)], moments_buf.at[s], more_sems.at[s]
        )
        for s, row in enumerate((DEPTH, rows - (side + 1) * DEPTH))
    ]
    for copy in weights:
        copy.start()
    words_ref[...] = middle_ref[...]
    bars.wait()
    for g in range(0, len(outer), PER_STEP):
        group = outer[g : g + PER_STEP]
        for copy in sum(copies[g : g + PER_STEP], []):
            copy.wait()
        pack(bar_ref, words_ref, spins_buf, draws_buf, group, g * DEPTH, False)
    inner = slice(LANES, columns - LANES)
    final_ref[:, inner] = sweeps_of([words_ref[w, :, inner] for w in range(WORDS)])
    for copy in weights:
        copy.wait()
    fill(
        (given_ref, kept_ref),
        odd_ref[0],
        lambda lower: [1 + i + (planes - side - 2) * lower for i in range(side)],
        lambda lower, i, t: moments_buf[
            lower, i * DEPTH : (i + 1) * DEPTH, pl.ds((t + 1) * TILE, TILE)
        ],
        lambda t: final_ref[:, pl.ds((t + 1) * TILE, TILE)],
    )


def widen_kernel(odd_ref, words_ref, beside_ref, across_ref, wide_ref, last_ref, first_ref, *, planes):
    columns = words_ref.shape[2]
    odd = odd_ref[0]
    lane = lax.broadcasted_iota(jnp.int32, (DEPTH, LANES), 1)
    beside, across = unstrips(beside_ref, DEPTH), unstrips(across_ref, DEPTH)
    for w in range(WORDS):
        wide_ref[w, :, LANES : LANES + columns] = words_ref[w]
        before = select(odd, beside[w], across[w])
        after = select(odd, across[w], beside[w])
        wide_ref[w, :, :LANES] = spread(before << (lane // 4))
        wide_ref[w, :, LANES + columns :] = spread(after << (lane // 4))
    for ref, top, place in ((last_ref, DEPTH - 8, planes), (first_ref, 0, 1)):
        bits = [(wide_ref[w, top : top + 8, :] >> place) & 1 for w in range(WORDS)]
        ref[...] = strips(codes(bits) + [jnp.zeros_like(bits[0])])


def side_kernel(
    odd_ref,
    wide_ref,
    above_ref,
    below_ref,
    moments_hbm,
    spins_ref,
    given_ref,
    kept_ref,
    joined_ref,
    tile_moments,
    row_moments,
    final_ref,
    sems,
):
    rows, columns = moments_hbm.shape
    planes = rows // DEPTH
    half = planes // 2
    side = half - MIDDLE
    weights = [
        pltpu.make_async_copy(
            moments_hbm.at[:, pl.ds(at, TILE)], tile_moments.at[s], sems.at[s]
        )
        for s, at in enumerate((0, columns - TILE))
    ] + [
        pltpu.make_async_copy(
            moments_hbm.at[pl.ds(at, DEPTH)], row_moments.at[s], sems.at[2 + s]
        )
        for s, at in enumerate((0, rows - DEPTH))
    ]
    for copy in weights:
        copy.start()
    above, below = unstrips(above_ref, 8), unstrips(below_ref, 8)
    joined_ref[...] = wide_ref[...]
    for w in range(WORDS):
        joined_ref[w, DEPTH - 8 :, :] = wide_ref[w, DEPTH - 8 :, :] | above[w]
        joined_ref[w, :8, :] = wide_ref[w, :8, :] | (below[w] << (planes + 1))
    final_ref[...] = sweeps_of([joined_ref[w] for w in range(WORDS)])
    spins_ref[...] = final_ref[:, LANES : LANES + columns]
    for copy in weights:
        copy.wait()
    odd = odd_ref[0]
    ends = (0, columns - TILE)
    for ref, lower in ((given_ref, 1 - odd), (kept_ref, odd)):
        for i in range(half):
            if i < side - 1:
                plane = 1 + i + (planes - side - 1) * lower
            elif i < half - 1:
                plane = 1 + i + MIDDLE * lower
            else:
                plane = (planes - 1) * lower
            at = pl.ds(pl.multiple_of(plane * DEPTH, DEPTH), DEPTH)
            for s, left in enumerate(ends):
                row = (s * half + i) * DEPTH
                ref[row : row + DEPTH, :] = weigh(
                    final_ref[:, LANES + left : LANES + left + TILE], tile_moments[s, at, :], plane
                )
        for t in range(1, columns // TILE - 1):
            row = (2 * half + t - 1) * DEPTH
            ref[row : row + DEPTH, :] = weigh(
                final_ref[:, LANES + t * TILE : LANES + (t + 1) * TILE],
                row_moments[lower, :, t * TILE : (t + 1) * TILE],
                (planes - 1) * lower,
            )


def spell_kernel(spins_ref, out_hbm, out_buf, sems):
    columns = spins_ref.shape[1]
    copies = []
    for plane in range(out_hbm.shape[0] // DEPTH):
        rows = pl.ds(plane * DEPTH, DEPTH)
        for left in range(0, columns, TILE):
            lanes = pl.ds(left, TILE)
            up = (spins_ref[:, lanes] & (1 << (plane + 1))) != 0
            out_buf[rows, lanes] = jnp.where(up, 1.0, -1.0)
        copies.append(pltpu.make_async_copy(out_buf.at[rows], out_hbm.at[rows], sems.at[plane]))
        copies[-1].start()
    for copy in copies:
        copy.wait()


def gram(left, right):
    return lax.dot_general(
        left, right, (((0,), (0,)), ((), ())), preferred_element_type=jnp.float32
    )


def stack(refs, first, last):
    return jnp.concatenate(
        [ref[first:last].reshape((last - first) * ref.shape[1], TILE) for ref in refs], axis=0
    )


def fold(sums_ref):
    width = R + LANES
    value = sums_ref[:LANES, :width] + sums_ref[LANES:, LANES : LANES + width]
    height = LANES // 2
    while height >= 8:
        value = value[:height] + pltpu.roll(value[height:], width - height, 1)
        height //= 2
    return value


def edge_rows(ends, tiles, first, last):
    start = ends.shape[0] - (tiles - 2) * DEPTH
    return ends[start + (first - 1) * DEPTH : start + (last - 1) * DEPTH, :]


def tile(block, t):
    low, high, ends = block
    tiles = low.shape[0] + 2
    height = low.shape[1] + high.shape[1] + DEPTH
    if t in (0, tiles - 1):
        return ends[min(t, 1) * height : (min(t, 1) + 1) * height, :]
    return jnp.concatenate([low[t - 1], high[t - 1], edge_rows(ends, tiles, t, t + 1)], axis=0)


def tiles_of(block, places):
    return jnp.concatenate([tile(block, t) for t in places], axis=0)


def own_kernel(*refs):
    parts, (out_ref, sums_ref) = refs[:-2], refs[-2:]
    blocks = (parts[:3], parts[3:])
    tiles = parts[0].shape[0] + 2
    for n in range(tiles):
        sums_ref[:, n * TILE : (n + 1) * TILE] = sum(
            gram(tiles_of(block, range(tiles - n)), tiles_of(block, range(n, tiles)))
            for block in blocks
        )
    sums_ref[:, tiles * TILE :] = jnp.zeros((TILE, TILE), jnp.float32)
    out_ref[...] = fold(sums_ref)


def by_side(odd_ref, own, mid, far, run):
    @pl.when(odd_ref[0] == 0)
    def _():
        run(((own, mid), (mid, far)))

    @pl.when(odd_ref[0] == 1)
    def _():
        run(((far, mid), (mid, own)))


def early_kernel(odd_ref, *refs):
    (base_ref, out_ref, sums_ref) = refs[-3:]
    tiles = refs[0].shape[0]
    sums_ref[:, : 3 * TILE] = jnp.zeros((TILE, 3 * TILE), jnp.float32)

    def run(pairs):
        for n in range(1, tiles + 1):
            sums_ref[:, (n + 2) * TILE : (n + 3) * TILE] = sum(
                gram(stack(left, tiles - n, tiles), stack(right, 0, n)) for left, right in pairs
            )

    by_side(odd_ref, refs[0:2], refs[2:4], refs[4:6], run)
    out_ref[...] = fold(sums_ref) + base_ref[...]


def late_kernel(scale, odd_ref, *refs):
    (base_ref, out_ref, sums_ref) = refs[-3:]
    tiles = refs[0].shape[0] + 2
    sums_ref[:, :TILE] = jnp.zeros((TILE, TILE), jnp.float32)

    def run(pairs):
        for n in range(1, tiles + 1):
            places = [(tiles - 1, n - 1)] + ([(tiles - n, 0)] if n > 1 else [])
            inner = n > 2
            sums_ref[:, n * TILE : (n + 1) * TILE] = sum(
                gram(
                    jnp.concatenate(
                        [tile(left, t) for t, _ in places]
                        + ([edge_rows(left[2], tiles, tiles + 1 - n, tiles - 1)] if inner else []),
                        axis=0,
                    ),
                    jnp.concatenate(
                        [tile(right, q) for _, q in places]
                        + ([edge_rows(right[2], tiles, 1, n - 1)] if inner else []),
                        axis=0,
                    ),
                )
                for left, right in pairs
            )

    by_side(odd_ref, refs[0:3], refs[3:6], refs[6:9], run)
    value = fold(sums_ref) + base_ref[...]
    for height in (4, 2, 1):
        value = value + pltpu.roll(pltpu.roll(value, value.shape[1] - height, 1), 8 - height, 0)
    value = value[:1] * scale
    share = out_ref.shape[2]
    for d in range(out_ref.shape[0]):
        out_ref[d] = value[:, d * share : (d + 1) * share]


def on_device(spins_up, uniforms, moments, accept_bar):
    rows, columns = spins_up.shape
    planes, tiles = rows // DEPTH, columns // TILE
    half_rows, half = rows // 2, planes // 2
    row_devices, col_devices = lax.axis_size("row"), lax.axis_size("col")
    devices = row_devices * col_devices
    assert columns == R and col_devices % 2 == 0 and planes % 2 == 0 and planes + 2 <= 26
    vmem = pl.BlockSpec(memory_space=pltpu.VMEM)
    smem = pl.BlockSpec(memory_space=pltpu.SMEM)
    anywhere = pl.BlockSpec(memory_space=pltpu.HBM)
    edge = jax.ShapeDtypeStruct((DEPTH * (1 + SWEEPS), LANES), jnp.bfloat16)
    words_shape = jax.ShapeDtypeStruct((WORDS, DEPTH, columns), jnp.int32)
    dma = pltpu.SemaphoreType.DMA
    odd = (lax.axis_index("col") % 2).reshape(1)
    moments = pltpu.with_memory_space_constraint(moments, pltpu.HBM)
    accept_bar = pltpu.with_memory_space_constraint(accept_bar, pltpu.HBM)

    def message(count, height):
        return jax.ShapeDtypeStruct((count, height, TILE), jnp.bfloat16)

    def ring(size, step):
        return [(i, (i + step) % size) for i in range(size)]

    def exchange(given, kept):
        beside = [(i, i ^ 1) for i in range(col_devices)]
        beyond = [(i, (i - 2 + 4 * (i % 2)) % col_devices) for i in range(col_devices)]
        return lax.ppermute(given, "col", beside), lax.ppermute(kept, "col", beyond)

    def call(kernel, specs, shapes, scratch, flops, moved, *operands):
        return pl.pallas_call(
            kernel,
            in_specs=specs,
            out_specs=jax.tree.map(lambda _: vmem, shapes),
            out_shape=shapes,
            scratch_shapes=scratch,
            compiler_params=params(),
            cost_estimate=pl.CostEstimate(flops=flops, bytes_accessed=moved, transcendentals=0),
        )(*operands)

    packed = (2 * MIDDLE + 2) * DEPTH
    remaining = rows - packed
    side = half - MIDDLE - 1
    middle = message(tiles - 2, MIDDLE * DEPTH)
    across_pairs = [(i, (i - 1 + 2 * (i % 2)) % col_devices) for i in range(col_devices)]
    beside_pairs = [(i, i ^ 1) for i in range(col_devices)]
    words, beside, across, given, kept = call(
        middle_kernel,
        [smem, anywhere, anywhere, anywhere, anywhere],
        [words_shape, edge, edge, middle, middle],
        [
            pltpu.VMEM((packed, columns), jnp.int32),
            pltpu.VMEM((SWEEPS, packed, columns), jnp.float32),
            pltpu.VMEM((4, remaining // 2, LANES), jnp.int32),
            pltpu.VMEM((SWEEPS, 4, remaining // 2, LANES), jnp.float32),
            pltpu.VMEM((2 * MIDDLE * DEPTH, columns), jnp.bfloat16),
            pltpu.VMEM((DEPTH, columns), jnp.int32),
            pltpu.SMEM((2,), jnp.float32),
            dma((pl.cdiv(2 * MIDDLE + 2, PER_STEP), 1 + SWEEPS)),
            dma((5, 1 + SWEEPS)),
        ],
        40 * packed * columns,
        4 * (1 + SWEEPS) * packed * columns,
        odd,
        accept_bar,
        spins_up,
        uniforms,
        moments,
    )
    own = [given, kept]
    got = [*exchange(given, kept)]
    beside = lax.ppermute(beside, "col", beside_pairs)
    across = lax.ppermute(across, "col", across_pairs)
    low = message(tiles - 2, side * DEPTH)
    words, given, kept = call(
        outer_kernel,
        [smem, anywhere, anywhere, anywhere, anywhere, vmem],
        [words_shape, low, low],
        [
            pltpu.VMEM((remaining, columns), jnp.int32),
            pltpu.VMEM((SWEEPS, remaining, columns), jnp.float32),
            pltpu.VMEM((2, side * DEPTH, columns), jnp.bfloat16),
            pltpu.VMEM((DEPTH, columns), jnp.int32),
            pltpu.SMEM((2,), jnp.float32),
            dma((remaining // DEPTH, 1 + SWEEPS)),
            dma((3,)),
        ],
        40 * remaining * columns,
        4 * (1 + SWEEPS) * remaining * columns,
        odd,
        accept_bar,
        spins_up,
        uniforms,
        moments,
        words,
    )
    own = [given, own[0], kept, own[1]]
    mid, far = exchange(given, kept)
    got = [mid, got[0], far, got[1]]
    wide_shape = jax.ShapeDtypeStruct((WORDS, DEPTH, columns + 2 * LANES), jnp.int32)
    strip = jax.ShapeDtypeStruct((8 * (2 + SWEEPS), columns + 2 * LANES), jnp.bfloat16)
    words, last, leading = call(
        functools.partial(widen_kernel, planes=planes),
        [smem, vmem, vmem, vmem],
        [wide_shape, strip, strip],
        [],
        20 * DEPTH * columns,
        40 * DEPTH * columns,
        odd,
        words,
        beside,
        across,
    )
    above = lax.ppermute(last, "row", ring(row_devices, 1))
    below = lax.ppermute(leading, "row", ring(row_devices, -1))
    ends = jax.ShapeDtypeStruct((2 * half_rows + (tiles - 2) * DEPTH, TILE), jnp.bfloat16)
    spins, given, kept = call(
        side_kernel,
        [smem, vmem, vmem, vmem, anywhere],
        [jax.ShapeDtypeStruct((DEPTH, columns), jnp.int32), ends, ends],
        [
            pltpu.VMEM(wide_shape.shape, jnp.int32),
            pltpu.VMEM((2, rows, TILE), jnp.bfloat16),
            pltpu.VMEM((2, DEPTH, columns), jnp.bfloat16),
            pltpu.VMEM(wide_shape.shape[1:], jnp.int32),
            dma((4,)),
        ],
        10 * rows * columns,
        rows * columns,
        odd,
        words,
        above,
        below,
        moments,
    )
    own = [own[0], own[1], given, own[2], own[3], kept]
    mid, far = exchange(given, kept)

    spins_out = pl.pallas_call(
        spell_kernel,
        in_specs=[vmem],
        out_specs=anywhere,
        out_shape=jax.ShapeDtypeStruct((rows, columns), jnp.float32),
        scratch_shapes=[pltpu.VMEM((rows, columns), jnp.float32), dma((planes,))],
        compiler_params=params(),
        cost_estimate=pl.CostEstimate(
            flops=rows * columns, bytes_accessed=4 * rows * columns, transcendentals=0
        ),
        name="spell",
    )(spins)
    normaliser = 1.0 / math.sqrt(rows * row_devices * columns * col_devices)
    sums = pltpu.VMEM((TILE, R + TILE), jnp.float32)
    folded = jax.ShapeDtypeStruct((8, R + LANES), jnp.float32)
    work = rows * columns * columns
    base = call(own_kernel, [vmem] * 6, folded, [sums], work, 2 * rows * columns, *own)
    base = call(
        early_kernel,
        [smem] + [vmem] * 7,
        folded,
        [sums],
        work // 2,
        2 * rows * columns,
        odd,
        own[3],
        own[4],
        *got,
        base,
    )
    partial_sums = call(
        functools.partial(late_kernel, normaliser),
        [smem] + [vmem] * 10,
        jax.ShapeDtypeStruct((devices, 1, R // devices), jnp.float32),
        [sums],
        work // 2,
        2 * rows * columns,
        odd,
        own[3],
        own[4],
        own[5],
        got[0],
        got[1],
        mid,
        got[2],
        got[3],
        far,
        base,
    )
    shares = lax.all_to_all(partial_sums, ("row", "col"), 0, 0, tiled=True)
    return spins_out, jnp.sum(shares, axis=(0, 1))


def solution(mesh):
    placed = (P("row", "col"), P(None, "row", "col"), P("row", "col"), P())
    return jax.shard_map(
        on_device,
        mesh=mesh,
        in_specs=placed,
        out_specs=(P("row", "col"), P(("row", "col"))),
        check_vma=False,
    )
```

```python
import functools
import math

import jax
import jax.numpy as jnp
from jax import lax
from jax.experimental import pallas as pl
from jax.experimental.pallas import tpu as pltpu
from jax.sharding import PartitionSpec as P

R = 2048
SWEEPS = 2
DEPTH = 32
LANES = 128
TILE = 256
PER_STEP = 2
MIDDLE = 6
WORDS = 1 + 2 * SWEEPS


def params(**more):
    return pltpu.CompilerParams(vmem_limit_bytes=48 << 20, **more)


def fetch(step, spins_hbm, draws_hbm, spins_buf, draws_buf, sems, row, at, count):
    copies = [
        pltpu.make_async_copy(
            spins_hbm.at[pl.ds(row, count)], spins_buf.at[pl.ds(at, count)], sems.at[step, 0]
        )
    ]
    for k in range(SWEEPS):
        copies.append(
            pltpu.make_async_copy(
                draws_hbm.at[k, pl.ds(row, count)],
                draws_buf.at[k, pl.ds(at, count)],
                sems.at[step, 1 + k],
            )
        )
    return copies


def pack(bar_ref, words_ref, spins_buf, draws_buf, planes, at, fresh):
    columns = words_ref.shape[2]
    for left in range(0, columns, TILE):
        lanes = pl.ds(left, TILE)
        if fresh:
            words = [jnp.zeros((DEPTH, TILE), jnp.int32)] * WORDS
        else:
            words = [words_ref[w, :, lanes] for w in range(WORDS)]
        for i, plane in enumerate(planes):
            bit = 1 << (plane + 1)
            rows = pl.ds(at + i * DEPTH, DEPTH)
            words[0] = words[0] | (spins_buf[rows, lanes] << (plane + 1))
            for k in range(SWEEPS):
                draw = draws_buf[k, rows, lanes]
                for c in range(2):
                    word = words[1 + 2 * k + c]
                    words[1 + 2 * k + c] = jnp.where(draw < bar_ref[c], word | bit, word)
        for w, word in enumerate(words):
            words_ref[w, :, lanes] = word


def groups_of(planes, size):
    return [planes[i : i + size] for i in range(0, len(planes), size)]


def strips(parts):
    return jnp.concatenate(parts, axis=0).astype(jnp.float32).astype(jnp.bfloat16)


def codes(bits):
    return [bits[0]] + [bits[1 + 2 * k] + 2 * bits[2 + 2 * k] for k in range(SWEEPS)]


def unstrips(ref, height):
    parts = [
        ref[k * height : (k + 1) * height, :].astype(jnp.float32).astype(jnp.int32)
        for k in range(1 + SWEEPS)
    ]
    bits = [parts[0]]
    for code in parts[1:]:
        bits += [code & 1, code >> 1]
    return bits


def spread(word):
    for shift in (4, 8, 16, 32, 64):
        word = word | pltpu.roll(word, shift, 1)
    return word


def sweeps_of(words):
    spins = words[0]
    width = spins.shape[1]
    row = lax.broadcasted_iota(jnp.int32, spins.shape, 0)
    parity = (row + lax.broadcasted_iota(jnp.int32, spins.shape, 1)) & 1
    for k in range(SWEEPS):
        for colour in range(2):
            up = pltpu.roll(spins, 1, 0)
            up = jnp.where(row == 0, up << 1, up)
            down = pltpu.roll(spins, DEPTH - 1, 0)
            down = jnp.where(row == DEPTH - 1, down >> 1, down)
            a, b = up ^ spins, down ^ spins
            c, d = pltpu.roll(spins, 1, 1) ^ spins, pltpu.roll(spins, width - 1, 1) ^ spins
            either, other = a | b, c | d
            some = either | other
            several = (a & b) | (c & d) | (either & other)
            flips = several | (some & words[1 + 2 * k]) | (words[2 + 2 * k] & ~some)
            spins = jnp.where(parity == colour, spins ^ flips, spins)
    return spins


def weigh(spins, moments, plane):
    up = (spins & (jnp.int32(1) << (plane + 1))) != 0
    return jnp.where(up, 1.0, -1.0).astype(jnp.bfloat16) * moments


def middle_kernel(
    odd_ref,
    bar_ref,
    spins_hbm,
    draws_hbm,
    moments_hbm,
    words_ref,
    last_ref,
    first_ref,
    given_ref,
    kept_ref,
    spins_buf,
    draws_buf,
    edge_spins,
    edge_draws,
    moments_buf,
    final_ref,
    bar_smem,
    sems,
    edge_sems,
):
    rows, columns = spins_hbm.shape
    half = rows // DEPTH // 2
    planes = list(range(half - MIDDLE - 1, half + MIDDLE + 1))
    top = planes[0] * DEPTH
    groups = groups_of(planes, PER_STEP)
    size = PER_STEP * DEPTH
    edges = [
        fetch(s, spins_hbm, draws_hbm, edge_spins, edge_draws, edge_sems, row, 8 * s, 8)
        for s, row in enumerate((rows - 8, 0))
    ]
    copies = [
        fetch(
            g,
            spins_hbm,
            draws_hbm,
            spins_buf,
            draws_buf,
            sems,
            top + g * size,
            g * size,
            len(group) * DEPTH,
        )
        for g, group in enumerate(groups)
    ]
    weights = pltpu.make_async_copy(
        moments_hbm.at[pl.ds((half - MIDDLE) * DEPTH, 2 * MIDDLE * DEPTH)],
        moments_buf,
        edge_sems.at[2, 0],
    )
    bars = pltpu.make_async_copy(bar_ref, bar_smem, edge_sems.at[2, 1])
    for copy in [bars] + sum(edges + copies, []) + [weights]:
        copy.start()
    bars.wait()
    bar_ref = bar_smem
    for s, ref in enumerate((last_ref, first_ref)):
        for copy in edges[s]:
            copy.wait()
        parts = [edge_spins[8 * s : 8 * s + 8, :]]
        for k in range(SWEEPS):
            draw = edge_draws[k, 8 * s : 8 * s + 8, :]
            one = (draw < bar_ref[0]).astype(jnp.int32)
            parts.append(one + 2 * (draw < bar_ref[1]).astype(jnp.int32))
        ref[...] = strips(parts + [jnp.zeros_like(parts[0])])
    for g, group in enumerate(groups):
        for copy in copies[g]:
            copy.wait()
        pack(bar_ref, words_ref, spins_buf, draws_buf, group, g * size, g == 0)
    inner = slice(LANES, columns - LANES)
    final_ref[:, inner] = sweeps_of([words_ref[w, :, inner] for w in range(WORDS)])
    weights.wait()
    for ref, lower in ((given_ref, 1 - odd_ref[0]), (kept_ref, odd_ref[0])):
        for i in range(MIDDLE):
            plane = half - MIDDLE + MIDDLE * lower + i
            at = pl.ds(pl.multiple_of((MIDDLE * lower + i) * DEPTH, DEPTH), DEPTH)
            for t in range(ref.shape[0]):
                lanes = pl.ds((t + 1) * TILE, TILE)
                ref[t, i * DEPTH : (i + 1) * DEPTH, :] = weigh(
                    final_ref[:, lanes], moments_buf[at, lanes], plane
                )


def outer_kernel(
    bar_ref,
    spins_hbm,
    draws_hbm,
    middle_ref,
    words_ref,
    spins_buf,
    draws_buf,
    bar_smem,
    sems,
    bar_sem,
):
    bars = pltpu.make_async_copy(bar_ref, bar_smem, bar_sem)
    bars.start()
    planes = spins_hbm.shape[0] // DEPTH
    side = planes // 2 - MIDDLE - 1
    outer = list(range(side)) + list(range(planes - side, planes))
    copies = []
    for g, plane in enumerate(outer):
        copies.append(
            fetch(
                g,
                spins_hbm,
                draws_hbm,
                spins_buf,
                draws_buf,
                sems,
                plane * DEPTH,
                g * DEPTH,
                DEPTH,
            )
        )
        for copy in copies[-1]:
            copy.start()
    words_ref[...] = middle_ref[...]
    bars.wait()
    bar_ref = bar_smem
    for g in range(0, len(outer), PER_STEP):
        group = outer[g : g + PER_STEP]
        for copy in sum(copies[g : g + PER_STEP], []):
            copy.wait()
        pack(bar_ref, words_ref, spins_buf, draws_buf, group, g * DEPTH, False)


def inner_kernel(
    odd_ref,
    words_ref,
    above_ref,
    below_ref,
    moments_hbm,
    spins_ref,
    sides_ref,
    right_ref,
    left_ref,
    given_ref,
    kept_ref,
    given_rest_ref,
    kept_rest_ref,
    joined_ref,
    moments_buf,
    sems,
):
    rows, columns = moments_hbm.shape
    planes = rows // DEPTH
    side = planes // 2 - MIDDLE
    weights = [
        pltpu.make_async_copy(
            moments_hbm.at[pl.ds(row, side * DEPTH)], moments_buf.at[s], sems.at[s]
        )
        for s, row in enumerate((0, rows - side * DEPTH))
    ]
    for copy in weights:
        copy.start()
    above, below = unstrips(above_ref, 8), unstrips(below_ref, 8)
    joined_ref[...] = words_ref[...]
    for w in range(WORDS):
        joined_ref[w, DEPTH - 8 :, :] = words_ref[w, DEPTH - 8 :, :] | above[w]
        joined_ref[w, :8, :] = words_ref[w, :8, :] | (below[w] << (planes + 1))
    lane = lax.broadcasted_iota(jnp.int32, (DEPTH, LANES), 1)
    for ref, at, held in (
        (right_ref, columns - LANES, lane >= LANES - 4),
        (left_ref, 0, lane < 4),
    ):
        bits = []
        for w in range(WORDS):
            edge = jnp.where(held, joined_ref[w, :, at : at + LANES], 0)
            bits.append((spread(edge) >> (lane // 4)) & 1)
        ref[...] = strips(codes(bits))
    reach = TILE + LANES
    sides_ref[:, :, :reach] = joined_ref[:, :, :reach]
    sides_ref[:, :, reach:] = joined_ref[:, :, columns - reach :]
    inner = slice(LANES, columns - LANES)
    spins_ref[:, :LANES] = jnp.zeros((DEPTH, LANES), jnp.int32)
    spins_ref[:, columns - LANES :] = jnp.zeros((DEPTH, LANES), jnp.int32)
    spins_ref[:, inner] = sweeps_of([joined_ref[w, :, inner] for w in range(WORDS)])
    for copy in weights:
        copy.wait()
    for ref, rest, lower in (
        (given_ref, given_rest_ref, 1 - odd_ref[0]),
        (kept_ref, kept_rest_ref, odd_ref[0]),
    ):
        for i in range(side):
            plane = (planes - side) * lower + i
            target = ref.at[:, pl.ds(i * DEPTH, DEPTH)] if i < side - 1 else rest
            for t in range(ref.shape[0]):
                lanes = pl.ds((t + 1) * TILE, TILE)
                target[t] = weigh(
                    spins_ref[:, lanes],
                    moments_buf[lower, i * DEPTH : (i + 1) * DEPTH, lanes],
                    plane,
                )


def side_kernel(
    odd_ref,
    sides_ref,
    before_ref,
    after_ref,
    moments_hbm,
    spins_ref,
    given_ref,
    kept_ref,
    moments_buf,
    final_ref,
    sems,
):
    rows, columns = moments_hbm.shape
    half = rows // DEPTH // 2
    weights = [
        pltpu.make_async_copy(
            moments_hbm.at[:, pl.ds(at, TILE)], moments_buf.at[s], sems.at[s]
        )
        for s, at in enumerate((0, columns - TILE))
    ]
    for copy in weights:
        copy.start()
    lane = lax.broadcasted_iota(jnp.int32, (DEPTH, LANES), 1)
    before, after = unstrips(before_ref, DEPTH), unstrips(after_ref, DEPTH)
    words = [
        jnp.concatenate(
            [spread(before[w] << (lane // 4)), sides_ref[w], spread(after[w] << (lane // 4))],
            axis=1,
        )
        for w in range(WORDS)
    ]
    updated = sweeps_of(words)
    width = updated.shape[1]
    final_ref[0] = updated[:, LANES : LANES + TILE]
    final_ref[1] = updated[:, width - LANES - TILE : width - LANES]
    spins_ref[...] = final_ref[...]
    for copy in weights:
        copy.wait()
    for ref, lower in ((given_ref, 1 - odd_ref[0]), (kept_ref, odd_ref[0])):
        for i in range(half):
            plane = i + lower * (half + MIDDLE if i < half - MIDDLE else MIDDLE)
            at = pl.ds(pl.multiple_of(plane * DEPTH, DEPTH), DEPTH)
            for s in range(2):
                ref[s, i * DEPTH : (i + 1) * DEPTH, :] = weigh(
                    final_ref[s], moments_buf[s, at, :], plane
                )


def spell_kernel(spins_ref, sides_ref, out_hbm, out_buf, sems):
    columns = spins_ref.shape[1]
    copies = []
    for plane in range(out_hbm.shape[0] // DEPTH):
        rows = pl.ds(plane * DEPTH, DEPTH)
        for left in range(0, columns, TILE):
            lanes = pl.ds(left, TILE)
            if left in (0, columns - TILE):
                word = sides_ref[min(left, 1)]
            else:
                word = spins_ref[:, lanes]
            up = (word & (1 << (plane + 1))) != 0
            out_buf[rows, lanes] = jnp.where(up, 1.0, -1.0)
        copies.append(pltpu.make_async_copy(out_buf.at[rows], out_hbm.at[rows], sems.at[plane]))
        copies[-1].start()
    for copy in copies:
        copy.wait()


def gram(left, right):
    return lax.dot_general(
        left, right, (((0,), (0,)), ((), ())), preferred_element_type=jnp.float32
    )


def stack(refs, first, last):
    return jnp.concatenate(
        [ref[first:last].reshape((last - first) * ref.shape[1], TILE) for ref in refs], axis=0
    )


def fold(sums_ref):
    width = R + LANES
    value = sums_ref[:LANES, :width] + sums_ref[LANES:, LANES : LANES + width]
    height = LANES // 2
    while height >= 8:
        value = value[:height] + pltpu.roll(value[height:], width - height, 1)
        height //= 2
    return value


def tile(block, t):
    parts, ends, rows = block
    last = parts[0].shape[0] + 1
    if t in (0, last):
        return jnp.concatenate([ends[min(t, 1), at] for at in rows], axis=0)
    return stack(parts, t - 1, t)


def tiles_of(block, places):
    return jnp.concatenate([tile(block, t) for t in places], axis=0)


def whole(parts):
    low, rest, high, ends = parts
    return (low, rest, high), ends, (slice(0, ends.shape[1]),)


def without_rest(parts):
    low, rest, high, ends = parts
    held = low.shape[1] + rest.shape[1]
    return (low, high), ends, (slice(0, low.shape[1]), slice(held, ends.shape[1]))


def rest_only(parts):
    low, rest, _, ends = parts
    return (rest,), ends, (slice(low.shape[1], low.shape[1] + rest.shape[1]),)


def own_kernel(*refs):
    parts, (out_ref, sums_ref) = refs[:-2], refs[-2:]
    blocks = (whole(parts[:4]), whole(parts[4:]))
    tiles = parts[0].shape[0] + 2
    for n in range(tiles):
        sums_ref[:, n * TILE : (n + 1) * TILE] = sum(
            gram(tiles_of(block, range(tiles - n)), tiles_of(block, range(n, tiles)))
            for block in blocks
        )
    sums_ref[:, tiles * TILE :] = jnp.zeros((TILE, TILE), jnp.float32)
    out_ref[...] = fold(sums_ref)


def by_side(odd_ref, own, mid, far, run):
    @pl.when(odd_ref[0] == 0)
    def _():
        run(((own, mid), (mid, far)))

    @pl.when(odd_ref[0] == 1)
    def _():
        run(((far, mid), (mid, own)))


def early_kernel(odd_ref, *refs):
    (base_ref, out_ref, sums_ref) = refs[-3:]
    tiles = refs[0].shape[0]
    sums_ref[:, : 3 * TILE] = jnp.zeros((TILE, 3 * TILE), jnp.float32)

    def run(pairs):
        for n in range(1, tiles + 1):
            sums_ref[:, (n + 2) * TILE : (n + 3) * TILE] = sum(
                gram(stack(left, tiles - n, tiles), stack(right, 0, n)) for left, right in pairs
            )

    by_side(odd_ref, refs[0:2], refs[2:4], refs[4:6], run)
    out_ref[...] = fold(sums_ref) + base_ref[...]


def late_kernel(odd_ref, *refs):
    (base_ref, out_ref, sums_ref) = refs[-3:]
    tiles = refs[0].shape[0] + 2
    sums_ref[:, :TILE] = jnp.zeros((TILE, TILE), jnp.float32)

    def run(pairs):
        pairs = [tuple(without_rest(part) for part in pair) for pair in pairs]
        for n in range(1, tiles + 1):
            places = [(tiles - 1, n - 1)] + ([(tiles - n, 0)] if n > 1 else [])
            sums_ref[:, n * TILE : (n + 1) * TILE] = sum(
                gram(tiles_of(left, [t for t, _ in places]), tiles_of(right, [q for _, q in places]))
                for left, right in pairs
            )

    by_side(odd_ref, refs[0:4], refs[4:8], refs[8:12], run)
    out_ref[...] = fold(sums_ref) + base_ref[...]


def last_kernel(scale, odd_ref, *refs):
    (base_ref, out_ref, sums_ref) = refs[-3:]
    tiles = refs[0].shape[0] + 2
    sums_ref[:, :TILE] = jnp.zeros((TILE, TILE), jnp.float32)

    def run(pairs):
        pairs = [tuple(rest_only(part) for part in pair) for pair in pairs]
        for n in range(1, tiles + 1):
            sums_ref[:, n * TILE : (n + 1) * TILE] = gram(
                jnp.concatenate(
                    [tiles_of(left, range(tiles - n, tiles)) for left, _ in pairs], axis=0
                ),
                jnp.concatenate([tiles_of(right, range(n)) for _, right in pairs], axis=0),
            )

    by_side(odd_ref, refs[0:4], refs[4:8], refs[8:12], run)
    value = fold(sums_ref) + base_ref[...]
    for height in (4, 2, 1):
        value = value + pltpu.roll(pltpu.roll(value, value.shape[1] - height, 1), 8 - height, 0)
    value = value[:1] * scale
    share = out_ref.shape[2]
    for d in range(out_ref.shape[0]):
        out_ref[d] = value[:, d * share : (d + 1) * share]


def on_device(spins_up, uniforms, moments, accept_bar):
    rows, columns = spins_up.shape
    planes, tiles = rows // DEPTH, columns // TILE
    half_rows, half = rows // 2, planes // 2
    row_devices, col_devices = lax.axis_size("row"), lax.axis_size("col")
    devices = row_devices * col_devices
    assert columns == R and col_devices % 2 == 0 and planes % 2 == 0 and planes + 2 <= 26
    vmem = pl.BlockSpec(memory_space=pltpu.VMEM)
    smem = pl.BlockSpec(memory_space=pltpu.SMEM)
    anywhere = pl.BlockSpec(memory_space=pltpu.HBM)
    strip = jax.ShapeDtypeStruct((8 * (2 + SWEEPS), columns), jnp.bfloat16)
    edge = jax.ShapeDtypeStruct((DEPTH * (1 + SWEEPS), LANES), jnp.bfloat16)
    words_shape = jax.ShapeDtypeStruct((WORDS, DEPTH, columns), jnp.int32)
    dma = pltpu.SemaphoreType.DMA
    odd = (lax.axis_index("col") % 2).reshape(1)
    moments = pltpu.with_memory_space_constraint(moments, pltpu.HBM)
    accept_bar = pltpu.with_memory_space_constraint(accept_bar, pltpu.HBM)

    def message(count, height):
        return jax.ShapeDtypeStruct((count, height, TILE), jnp.bfloat16)

    def ring(size, step):
        return [(i, (i + step) % size) for i in range(size)]

    def exchange(given, kept):
        beside = [(i, i ^ 1) for i in range(col_devices)]
        beyond = [(i, (i - 2 + 4 * (i % 2)) % col_devices) for i in range(col_devices)]
        return lax.ppermute(given, "col", beside), lax.ppermute(kept, "col", beyond)

    def call(kernel, specs, shapes, scratch, flops, moved, *operands):
        return pl.pallas_call(
            kernel,
            in_specs=specs,
            out_specs=jax.tree.map(lambda _: vmem, shapes),
            out_shape=shapes,
            scratch_shapes=scratch,
            compiler_params=params(),
            cost_estimate=pl.CostEstimate(flops=flops, bytes_accessed=moved, transcendentals=0),
        )(*operands)

    packed = (2 * MIDDLE + 2) * DEPTH
    middle = message(tiles - 2, MIDDLE * DEPTH)
    words, last, leading, given, kept = call(
        middle_kernel,
        [smem, anywhere, anywhere, anywhere, anywhere],
        [words_shape, strip, strip, middle, middle],
        [
            pltpu.VMEM((packed, columns), jnp.int32),
            pltpu.VMEM((SWEEPS, packed, columns), jnp.float32),
            pltpu.VMEM((16, columns), jnp.int32),
            pltpu.VMEM((SWEEPS, 16, columns), jnp.float32),
            pltpu.VMEM((2 * MIDDLE * DEPTH, columns), jnp.bfloat16),
            pltpu.VMEM((DEPTH, columns), jnp.int32),
            pltpu.SMEM((2,), jnp.float32),
            dma((pl.cdiv(2 * MIDDLE + 2, PER_STEP), 1 + SWEEPS)),
            dma((3, 1 + SWEEPS)),
        ],
        40 * packed * columns,
        4 * (1 + SWEEPS) * packed * columns,
        odd,
        accept_bar,
        spins_up,
        uniforms,
        moments,
    )
    own = [given, kept]
    got = [*exchange(given, kept)]
    above = lax.ppermute(last, "row", ring(row_devices, 1))
    below = lax.ppermute(leading, "row", ring(row_devices, -1))

    remaining = rows - packed
    words = call(
        outer_kernel,
        [anywhere, anywhere, anywhere, vmem],
        words_shape,
        [
            pltpu.VMEM((remaining, columns), jnp.int32),
            pltpu.VMEM((SWEEPS, remaining, columns), jnp.float32),
            pltpu.SMEM((2,), jnp.float32),
            dma((remaining // DEPTH, 1 + SWEEPS)),
            dma(()),
        ],
        40 * remaining * columns,
        4 * (1 + SWEEPS) * remaining * columns,
        accept_bar,
        spins_up,
        uniforms,
        words,
    )
    side = half - MIDDLE
    low, rest = message(tiles - 2, (side - 1) * DEPTH), message(tiles - 2, DEPTH)
    reach = 2 * (TILE + LANES)
    spins, sides, right, left, given, kept, given_rest, kept_rest = call(
        inner_kernel,
        [smem, vmem, vmem, vmem, anywhere],
        [
            jax.ShapeDtypeStruct((DEPTH, columns), jnp.int32),
            jax.ShapeDtypeStruct((WORDS, DEPTH, reach), jnp.int32),
            edge,
            edge,
            low,
            low,
            rest,
            rest,
        ],
        [
            pltpu.VMEM(words_shape.shape, jnp.int32),
            pltpu.VMEM((2, side * DEPTH, columns), jnp.bfloat16),
            dma((2,)),
        ],
        40 * rows * columns,
        4 * rows * columns,
        odd,
        words,
        above,
        below,
        moments,
    )
    mid, far = exchange(given, kept)
    given, kept = [given, given_rest, own[0]], [kept, kept_rest, own[1]]
    got = [[mid, got[0]], [far, got[1]]]
    before = lax.ppermute(right, "col", ring(col_devices, 1))
    after = lax.ppermute(left, "col", ring(col_devices, -1))
    ends = message(2, half_rows)
    side_spins, given_ends, kept_ends = call(
        side_kernel,
        [smem, vmem, vmem, vmem, anywhere],
        [jax.ShapeDtypeStruct((2, DEPTH, TILE), jnp.int32), ends, ends],
        [
            pltpu.VMEM((2, rows, TILE), jnp.bfloat16),
            pltpu.VMEM((2, DEPTH, TILE), jnp.int32),
            dma((2,)),
        ],
        10 * rows * columns,
        rows * columns,
        odd,
        sides,
        before,
        after,
        moments,
    )
    given, kept = given + [given_ends], kept + [kept_ends]
    mid_ends, far_ends = exchange(given_ends, kept_ends)
    mid_rest, far_rest = exchange(given_rest, kept_rest)

    spins_out = pl.pallas_call(
        spell_kernel,
        in_specs=[vmem, vmem],
        out_specs=anywhere,
        out_shape=jax.ShapeDtypeStruct((rows, columns), jnp.float32),
        scratch_shapes=[pltpu.VMEM((rows, columns), jnp.float32), dma((planes,))],
        compiler_params=params(),
        cost_estimate=pl.CostEstimate(
            flops=rows * columns, bytes_accessed=4 * rows * columns, transcendentals=0
        ),
        name="spell",
    )(spins, side_spins)
    normaliser = 1.0 / math.sqrt(rows * row_devices * columns * col_devices)
    sums = pltpu.VMEM((TILE, R + TILE), jnp.float32)
    folded = jax.ShapeDtypeStruct((8, R + LANES), jnp.float32)
    work = rows * columns * columns
    base = call(own_kernel, [vmem] * 8, folded, [sums], work, 2 * rows * columns, *given, *kept)
    base = call(
        early_kernel,
        [smem] + [vmem] * 7,
        folded,
        [sums],
        work // 2,
        2 * rows * columns,
        odd,
        kept[0],
        kept[2],
        *got[0],
        *got[1],
        base,
    )
    base = call(
        late_kernel,
        [smem] + [vmem] * 13,
        folded,
        [sums],
        work // 2,
        2 * rows * columns,
        odd,
        *kept,
        got[0][0],
        given_rest,
        got[0][1],
        mid_ends,
        got[1][0],
        kept_rest,
        got[1][1],
        far_ends,
        base,
    )
    partial_sums = call(
        functools.partial(last_kernel, normaliser),
        [smem] + [vmem] * 13,
        jax.ShapeDtypeStruct((devices, 1, R // devices), jnp.float32),
        [sums],
        work // 8,
        rows * columns,
        odd,
        *kept,
        got[0][0],
        mid_rest,
        got[0][1],
        mid_ends,
        got[1][0],
        far_rest,
        got[1][1],
        far_ends,
        base,
    )
    shares = lax.all_to_all(partial_sums, ("row", "col"), 0, 0, tiled=True)
    return spins_out, jnp.sum(shares, axis=(0, 1))


def solution(mesh):
    placed = (P("row", "col"), P(None, "row", "col"), P("row", "col"), P())
    return jax.shard_map(
        on_device,
        mesh=mesh,
        in_specs=placed,
        out_specs=(P("row", "col"), P(("row", "col"))),
        check_vma=False,
    )
```

```python
import functools
import math

import jax
import jax.numpy as jnp
from jax import lax
from jax.experimental import pallas as pl
from jax.experimental.pallas import tpu as pltpu
from jax.sharding import PartitionSpec as P

R = 2048
SWEEPS = 2
DEPTH = 32
LANES = 128
TILE = 256
PER_STEP = 2
MIDDLE = 5
WORDS = 1 + 2 * SWEEPS


def params(**more):
    return pltpu.CompilerParams(vmem_limit_bytes=48 << 20, **more)


def fetch(step, spins_hbm, draws_hbm, spins_buf, draws_buf, sems, row, at, count):
    copies = [
        pltpu.make_async_copy(
            spins_hbm.at[pl.ds(row, count)], spins_buf.at[pl.ds(at, count)], sems.at[step, 0]
        )
    ]
    for k in range(SWEEPS):
        copies.append(
            pltpu.make_async_copy(
                draws_hbm.at[k, pl.ds(row, count)],
                draws_buf.at[k, pl.ds(at, count)],
                sems.at[step, 1 + k],
            )
        )
    return copies


def pack(bar_ref, words_ref, spins_buf, draws_buf, planes, at, fresh):
    columns = words_ref.shape[2]
    for left in range(0, columns, TILE):
        lanes = pl.ds(left, TILE)
        if fresh:
            words = [jnp.zeros((DEPTH, TILE), jnp.int32)] * WORDS
        else:
            words = [words_ref[w, :, lanes] for w in range(WORDS)]
        for i, plane in enumerate(planes):
            bit = 1 << (plane + 1)
            rows = pl.ds(at + i * DEPTH, DEPTH)
            words[0] = words[0] | (spins_buf[rows, lanes] << (plane + 1))
            for k in range(SWEEPS):
                draw = draws_buf[k, rows, lanes]
                for c in range(2):
                    word = words[1 + 2 * k + c]
                    words[1 + 2 * k + c] = jnp.where(draw < bar_ref[c], word | bit, word)
        for w, word in enumerate(words):
            words_ref[w, :, lanes] = word


def groups_of(planes, size):
    return [planes[i : i + size] for i in range(0, len(planes), size)]


def strips(parts):
    return jnp.concatenate(parts, axis=0).astype(jnp.float32).astype(jnp.bfloat16)


def codes(bits):
    return [bits[0]] + [bits[1 + 2 * k] + 2 * bits[2 + 2 * k] for k in range(SWEEPS)]


def unstrips(ref, height):
    parts = [
        ref[k * height : (k + 1) * height, :].astype(jnp.float32).astype(jnp.int32)
        for k in range(1 + SWEEPS)
    ]
    bits = [parts[0]]
    for code in parts[1:]:
        bits += [code & 1, code >> 1]
    return bits


def spread(word):
    for shift in (4, 8, 16, 32, 64):
        word = word | pltpu.roll(word, shift, 1)
    return word


def sweeps_of(words):
    spins = words[0]
    width = spins.shape[1]
    row = lax.broadcasted_iota(jnp.int32, spins.shape, 0)
    parity = (row + lax.broadcasted_iota(jnp.int32, spins.shape, 1)) & 1
    for k in range(SWEEPS):
        for colour in range(2):
            up = pltpu.roll(spins, 1, 0)
            up = jnp.where(row == 0, up << 1, up)
            down = pltpu.roll(spins, DEPTH - 1, 0)
            down = jnp.where(row == DEPTH - 1, down >> 1, down)
            a, b = up ^ spins, down ^ spins
            c, d = pltpu.roll(spins, 1, 1) ^ spins, pltpu.roll(spins, width - 1, 1) ^ spins
            either, other = a | b, c | d
            some = either | other
            several = (a & b) | (c & d) | (either & other)
            flips = several | (some & words[1 + 2 * k]) | (words[2 + 2 * k] & ~some)
            spins = jnp.where(parity == colour, spins ^ flips, spins)
    return spins


def weigh(spins, moments, plane):
    up = (spins & (jnp.int32(1) << (plane + 1))) != 0
    return jnp.where(up, 1.0, -1.0).astype(jnp.bfloat16) * moments


def select(odd, when_odd, when_even):
    return jnp.where(odd == 1, when_odd, when_even)


def fill(refs, odd, planes_of, moments_of, spins_of):
    for ref, lower in zip(refs, (1 - odd, odd)):
        for i, plane in enumerate(planes_of(lower)):
            for t in range(ref.shape[0]):
                ref[t, i * DEPTH : (i + 1) * DEPTH, :] = weigh(
                    spins_of(t), moments_of(lower, i, t), plane
                )


def middle_kernel(
    odd_ref,
    bar_ref,
    spins_hbm,
    draws_hbm,
    moments_hbm,
    words_ref,
    last_ref,
    first_ref,
    given_ref,
    kept_ref,
    spins_buf,
    draws_buf,
    edge_spins,
    edge_draws,
    moments_buf,
    final_ref,
    bar_smem,
    sems,
    edge_sems,
):
    rows, columns = spins_hbm.shape
    half = rows // DEPTH // 2
    planes = list(range(half - MIDDLE - 1, half + MIDDLE + 1))
    top = planes[0] * DEPTH
    groups = groups_of(planes, 2 * PER_STEP)
    size = 2 * PER_STEP * DEPTH
    edges = [
        fetch(s, spins_hbm, draws_hbm, edge_spins, edge_draws, edge_sems, row, 8 * s, 8)
        for s, row in enumerate((rows - 8, 0))
    ]
    copies = [
        fetch(
            g,
            spins_hbm,
            draws_hbm,
            spins_buf,
            draws_buf,
            sems,
            top + g * size,
            g * size,
            len(group) * DEPTH,
        )
        for g, group in enumerate(groups)
    ]
    weights = pltpu.make_async_copy(
        moments_hbm.at[pl.ds((half - MIDDLE) * DEPTH, 2 * MIDDLE * DEPTH)],
        moments_buf,
        edge_sems.at[2, 0],
    )
    bars = pltpu.make_async_copy(bar_ref, bar_smem, edge_sems.at[2, 1])
    for copy in [bars] + sum(edges + copies, []) + [weights]:
        copy.start()
    bars.wait()
    bar_ref = bar_smem
    for s, ref in enumerate((last_ref, first_ref)):
        for copy in edges[s]:
            copy.wait()
        parts = [edge_spins[8 * s : 8 * s + 8, :]]
        for k in range(SWEEPS):
            draw = edge_draws[k, 8 * s : 8 * s + 8, :]
            one = (draw < bar_ref[0]).astype(jnp.int32)
            parts.append(one + 2 * (draw < bar_ref[1]).astype(jnp.int32))
        ref[...] = strips(parts + [jnp.zeros_like(parts[0])])
    for g, group in enumerate(groups):
        for copy in copies[g]:
            copy.wait()
        pack(bar_ref, words_ref, spins_buf, draws_buf, group, g * size, g == 0)
    inner = slice(LANES, columns - LANES)
    final_ref[:, inner] = sweeps_of([words_ref[w, :, inner] for w in range(WORDS)])
    weights.wait()
    for ref, lower in ((given_ref, 1 - odd_ref[0]), (kept_ref, odd_ref[0])):
        for i in range(MIDDLE):
            plane = half - MIDDLE + MIDDLE * lower + i
            at = pl.ds(pl.multiple_of((MIDDLE * lower + i) * DEPTH, DEPTH), DEPTH)
            for t in range(ref.shape[0]):
                lanes = pl.ds((t + 1) * TILE, TILE)
                ref[t, i * DEPTH : (i + 1) * DEPTH, :] = weigh(
                    final_ref[:, lanes], moments_buf[at, lanes], plane
                )


def outer_kernel(
    odd_ref,
    bar_hbm,
    spins_hbm,
    draws_hbm,
    moments_hbm,
    middle_ref,
    words_ref,
    given_ref,
    kept_ref,
    spins_buf,
    draws_buf,
    moments_buf,
    final_ref,
    bar_ref,
    sems,
    more_sems,
):
    rows, columns = spins_hbm.shape
    planes = rows // DEPTH
    side = planes // 2 - MIDDLE - 1
    outer = list(range(side)) + list(range(planes - side, planes))
    bars = pltpu.make_async_copy(bar_hbm, bar_ref, more_sems.at[2])
    bars.start()
    copies = []
    for g, plane in enumerate(outer):
        copies.append(
            fetch(
                g,
                spins_hbm,
                draws_hbm,
                spins_buf,
                draws_buf,
                sems,
                plane * DEPTH,
                g * DEPTH,
                DEPTH,
            )
        )
        for copy in copies[-1]:
            copy.start()
    weights = [
        pltpu.make_async_copy(
            moments_hbm.at[pl.ds(row, side * DEPTH)], moments_buf.at[s], more_sems.at[s]
        )
        for s, row in enumerate((DEPTH, rows - (side + 1) * DEPTH))
    ]
    for copy in weights:
        copy.start()
    words_ref[...] = middle_ref[...]
    bars.wait()
    for g in range(0, len(outer), PER_STEP):
        group = outer[g : g + PER_STEP]
        for copy in sum(copies[g : g + PER_STEP], []):
            copy.wait()
        pack(bar_ref, words_ref, spins_buf, draws_buf, group, g * DEPTH, False)
    inner = slice(LANES, columns - LANES)
    final_ref[:, inner] = sweeps_of([words_ref[w, :, inner] for w in range(WORDS)])
    for copy in weights:
        copy.wait()
    fill(
        (given_ref, kept_ref),
        odd_ref[0],
        lambda lower: [1 + i + (planes - side - 2) * lower for i in range(side)],
        lambda lower, i, t: moments_buf[
            lower, i * DEPTH : (i + 1) * DEPTH, pl.ds((t + 1) * TILE, TILE)
        ],
        lambda t: final_ref[:, pl.ds((t + 1) * TILE, TILE)],
    )


def join_kernel(odd_ref, words_ref, above_ref, below_ref, joined_ref, beside_ref, across_ref, *, planes):
    columns = words_ref.shape[2]
    above, below = unstrips(above_ref, 8), unstrips(below_ref, 8)
    joined_ref[...] = words_ref[...]
    for w in range(WORDS):
        joined_ref[w, DEPTH - 8 :, :] = words_ref[w, DEPTH - 8 :, :] | above[w]
        joined_ref[w, :8, :] = words_ref[w, :8, :] | (below[w] << (planes + 1))
    lane = lax.broadcasted_iota(jnp.int32, (DEPTH, LANES), 1)
    sent = []
    for at, held in ((columns - LANES, lane >= LANES - 4), (0, lane < 4)):
        bits = []
        for w in range(WORDS):
            edge = jnp.where(held, joined_ref[w, :, at : at + LANES], 0)
            bits.append((spread(edge) >> (lane // 4)) & 1)
        sent.append(jnp.concatenate(codes(bits), axis=0).astype(jnp.float32))
    odd = odd_ref[0]
    beside_ref[...] = select(odd, sent[1], sent[0]).astype(jnp.bfloat16)
    across_ref[...] = select(odd, sent[0], sent[1]).astype(jnp.bfloat16)


def side_kernel(
    odd_ref,
    joined_ref,
    beside_ref,
    across_ref,
    moments_hbm,
    spins_ref,
    given_ref,
    kept_ref,
    tile_moments,
    row_moments,
    final_ref,
    sems,
):
    rows, columns = moments_hbm.shape
    planes = rows // DEPTH
    half = planes // 2
    side = half - MIDDLE
    weights = [
        pltpu.make_async_copy(
            moments_hbm.at[:, pl.ds(at, TILE)], tile_moments.at[s], sems.at[s]
        )
        for s, at in enumerate((0, columns - TILE))
    ] + [
        pltpu.make_async_copy(
            moments_hbm.at[pl.ds(at, DEPTH)], row_moments.at[s], sems.at[2 + s]
        )
        for s, at in enumerate((0, rows - DEPTH))
    ]
    for copy in weights:
        copy.start()
    lane = lax.broadcasted_iota(jnp.int32, (DEPTH, LANES), 1)
    odd = odd_ref[0]
    words = []
    for w, halos in enumerate(zip(unstrips(beside_ref, DEPTH), unstrips(across_ref, DEPTH))):
        before, after = select(odd, *halos), select(odd, *halos[::-1])
        words.append(
            jnp.concatenate(
                [spread(before << (lane // 4)), joined_ref[w], spread(after << (lane // 4))],
                axis=1,
            )
        )
    final_ref[...] = sweeps_of(words)
    spins_ref[...] = final_ref[:, LANES : LANES + columns]
    for copy in weights:
        copy.wait()
    odd = odd_ref[0]
    ends = (0, columns - TILE)
    for ref, lower in ((given_ref, 1 - odd), (kept_ref, odd)):
        for i in range(half):
            if i < side - 1:
                plane = 1 + i + (planes - side - 1) * lower
            elif i < half - 1:
                plane = 1 + i + MIDDLE * lower
            else:
                plane = (planes - 1) * lower
            at = pl.ds(pl.multiple_of(plane * DEPTH, DEPTH), DEPTH)
            for s, left in enumerate(ends):
                row = (s * half + i) * DEPTH
                ref[row : row + DEPTH, :] = weigh(
                    final_ref[:, LANES + left : LANES + left + TILE], tile_moments[s, at, :], plane
                )
        for t in range(1, columns // TILE - 1):
            row = (2 * half + t - 1) * DEPTH
            ref[row : row + DEPTH, :] = weigh(
                final_ref[:, LANES + t * TILE : LANES + (t + 1) * TILE],
                row_moments[lower, :, t * TILE : (t + 1) * TILE],
                (planes - 1) * lower,
            )


def spell_kernel(spins_ref, out_hbm, out_buf, sems):
    columns = spins_ref.shape[1]
    copies = []
    for plane in range(out_hbm.shape[0] // DEPTH):
        rows = pl.ds(plane * DEPTH, DEPTH)
        for left in range(0, columns, TILE):
            lanes = pl.ds(left, TILE)
            up = (spins_ref[:, lanes] & (1 << (plane + 1))) != 0
            out_buf[rows, lanes] = jnp.where(up, 1.0, -1.0)
        copies.append(pltpu.make_async_copy(out_buf.at[rows], out_hbm.at[rows], sems.at[plane]))
        copies[-1].start()
    for copy in copies:
        copy.wait()


def gram(left, right):
    return lax.dot_general(
        left, right, (((0,), (0,)), ((), ())), preferred_element_type=jnp.float32
    )


def stack(refs, first, last):
    return jnp.concatenate(
        [ref[first:last].reshape((last - first) * ref.shape[1], TILE) for ref in refs], axis=0
    )


def fold(sums_ref):
    width = R + LANES
    value = sums_ref[:LANES, :width] + sums_ref[LANES:, LANES : LANES + width]
    height = LANES // 2
    while height >= 8:
        value = value[:height] + pltpu.roll(value[height:], width - height, 1)
        height //= 2
    return value


def edge_rows(ends, tiles, first, last):
    start = ends.shape[0] - (tiles - 2) * DEPTH
    return ends[start + (first - 1) * DEPTH : start + (last - 1) * DEPTH, :]


def tile(block, t):
    low, high, ends = block
    tiles = low.shape[0] + 2
    height = low.shape[1] + high.shape[1] + DEPTH
    if t in (0, tiles - 1):
        return ends[min(t, 1) * height : (min(t, 1) + 1) * height, :]
    return jnp.concatenate([low[t - 1], high[t - 1], edge_rows(ends, tiles, t, t + 1)], axis=0)


def tiles_of(block, places):
    return jnp.concatenate([tile(block, t) for t in places], axis=0)


def own_kernel(*refs):
    parts, (out_ref, sums_ref) = refs[:-2], refs[-2:]
    blocks = (parts[:3], parts[3:])
    tiles = parts[0].shape[0] + 2
    for n in range(tiles):
        sums_ref[:, n * TILE : (n + 1) * TILE] = sum(
            gram(tiles_of(block, range(tiles - n)), tiles_of(block, range(n, tiles)))
            for block in blocks
        )
    sums_ref[:, tiles * TILE :] = jnp.zeros((TILE, TILE), jnp.float32)
    out_ref[...] = fold(sums_ref)


def by_side(odd_ref, own, mid, far, run):
    @pl.when(odd_ref[0] == 0)
    def _():
        run(((own, mid), (mid, far)))

    @pl.when(odd_ref[0] == 1)
    def _():
        run(((far, mid), (mid, own)))


def early_kernel(odd_ref, *refs):
    (base_ref, out_ref, sums_ref) = refs[-3:]
    tiles = refs[0].shape[0]
    sums_ref[:, : 3 * TILE] = jnp.zeros((TILE, 3 * TILE), jnp.float32)

    def run(pairs):
        for n in range(1, tiles + 1):
            sums_ref[:, (n + 2) * TILE : (n + 3) * TILE] = sum(
                gram(stack(left, tiles - n, tiles), stack(right, 0, n)) for left, right in pairs
            )

    by_side(odd_ref, refs[0:2], refs[2:4], refs[4:6], run)
    out_ref[...] = fold(sums_ref) + base_ref[...]


def late_kernel(scale, odd_ref, *refs):
    (base_ref, out_ref, sums_ref) = refs[-3:]
    tiles = refs[0].shape[0] + 2
    sums_ref[:, :TILE] = jnp.zeros((TILE, TILE), jnp.float32)

    def run(pairs):
        for n in range(1, tiles + 1):
            places = [(tiles - 1, n - 1)] + ([(tiles - n, 0)] if n > 1 else [])
            inner = n > 2
            sums_ref[:, n * TILE : (n + 1) * TILE] = sum(
                gram(
                    jnp.concatenate(
                        [tile(left, t) for t, _ in places]
                        + ([edge_rows(left[2], tiles, tiles + 1 - n, tiles - 1)] if inner else []),
                        axis=0,
                    ),
                    jnp.concatenate(
                        [tile(right, q) for _, q in places]
                        + ([edge_rows(right[2], tiles, 1, n - 1)] if inner else []),
                        axis=0,
                    ),
                )
                for left, right in pairs
            )

    by_side(odd_ref, refs[0:3], refs[3:6], refs[6:9], run)
    value = fold(sums_ref) + base_ref[...]
    for height in (4, 2, 1):
        value = value + pltpu.roll(pltpu.roll(value, value.shape[1] - height, 1), 8 - height, 0)
    value = value[:1] * scale
    share = out_ref.shape[2]
    for d in range(out_ref.shape[0]):
        out_ref[d] = value[:, d * share : (d + 1) * share]


def on_device(spins_up, uniforms, moments, accept_bar):
    rows, columns = spins_up.shape
    planes, tiles = rows // DEPTH, columns // TILE
    half_rows, half = rows // 2, planes // 2
    row_devices, col_devices = lax.axis_size("row"), lax.axis_size("col")
    devices = row_devices * col_devices
    assert columns == R and col_devices % 2 == 0 and planes % 2 == 0 and planes + 2 <= 26
    vmem = pl.BlockSpec(memory_space=pltpu.VMEM)
    smem = pl.BlockSpec(memory_space=pltpu.SMEM)
    anywhere = pl.BlockSpec(memory_space=pltpu.HBM)
    strip = jax.ShapeDtypeStruct((8 * (2 + SWEEPS), columns), jnp.bfloat16)
    edge = jax.ShapeDtypeStruct((DEPTH * (1 + SWEEPS), LANES), jnp.bfloat16)
    words_shape = jax.ShapeDtypeStruct((WORDS, DEPTH, columns), jnp.int32)
    dma = pltpu.SemaphoreType.DMA
    odd = (lax.axis_index("col") % 2).reshape(1)
    moments = pltpu.with_memory_space_constraint(moments, pltpu.HBM)
    accept_bar = pltpu.with_memory_space_constraint(accept_bar, pltpu.HBM)

    def message(count, height):
        return jax.ShapeDtypeStruct((count, height, TILE), jnp.bfloat16)

    def ring(size, step):
        return [(i, (i + step) % size) for i in range(size)]

    def exchange(given, kept):
        beside = [(i, i ^ 1) for i in range(col_devices)]
        beyond = [(i, (i - 2 + 4 * (i % 2)) % col_devices) for i in range(col_devices)]
        return lax.ppermute(given, "col", beside), lax.ppermute(kept, "col", beyond)

    def call(kernel, specs, shapes, scratch, flops, moved, *operands):
        return pl.pallas_call(
            kernel,
            in_specs=specs,
            out_specs=jax.tree.map(lambda _: vmem, shapes),
            out_shape=shapes,
            scratch_shapes=scratch,
            compiler_params=params(),
            cost_estimate=pl.CostEstimate(flops=flops, bytes_accessed=moved, transcendentals=0),
        )(*operands)

    packed = (2 * MIDDLE + 2) * DEPTH
    remaining = rows - packed
    side = half - MIDDLE - 1
    middle = message(tiles - 2, MIDDLE * DEPTH)
    words, last, leading, given, kept = call(
        middle_kernel,
        [smem, anywhere, anywhere, anywhere, anywhere],
        [words_shape, strip, strip, middle, middle],
        [
            pltpu.VMEM((packed, columns), jnp.int32),
            pltpu.VMEM((SWEEPS, packed, columns), jnp.float32),
            pltpu.VMEM((16, columns), jnp.int32),
            pltpu.VMEM((SWEEPS, 16, columns), jnp.float32),
            pltpu.VMEM((2 * MIDDLE * DEPTH, columns), jnp.bfloat16),
            pltpu.VMEM((DEPTH, columns), jnp.int32),
            pltpu.SMEM((2,), jnp.float32),
            dma((pl.cdiv(2 * MIDDLE + 2, 2 * PER_STEP), 1 + SWEEPS)),
            dma((3, 1 + SWEEPS)),
        ],
        40 * packed * columns,
        4 * (1 + SWEEPS) * packed * columns,
        odd,
        accept_bar,
        spins_up,
        uniforms,
        moments,
    )
    own = [given, kept]
    got = [*exchange(given, kept)]
    above = lax.ppermute(last, "row", ring(row_devices, 1))
    below = lax.ppermute(leading, "row", ring(row_devices, -1))
    low = message(tiles - 2, side * DEPTH)
    words, given, kept = call(
        outer_kernel,
        [smem, anywhere, anywhere, anywhere, anywhere, vmem],
        [words_shape, low, low],
        [
            pltpu.VMEM((remaining, columns), jnp.int32),
            pltpu.VMEM((SWEEPS, remaining, columns), jnp.float32),
            pltpu.VMEM((2, side * DEPTH, columns), jnp.bfloat16),
            pltpu.VMEM((DEPTH, columns), jnp.int32),
            pltpu.SMEM((2,), jnp.float32),
            dma((remaining // DEPTH, 1 + SWEEPS)),
            dma((3,)),
        ],
        40 * remaining * columns,
        4 * (1 + SWEEPS) * remaining * columns,
        odd,
        accept_bar,
        spins_up,
        uniforms,
        moments,
        words,
    )
    own = [given, own[0], kept, own[1]]
    mid, far = exchange(given, kept)
    got = [mid, got[0], far, got[1]]
    joined, beside, across = call(
        functools.partial(join_kernel, planes=planes),
        [smem, vmem, vmem, vmem],
        [words_shape, edge, edge],
        [],
        20 * DEPTH * columns,
        40 * DEPTH * columns,
        odd,
        words,
        above,
        below,
    )
    across = lax.ppermute(
        across, "col", [(i, (i - 1 + 2 * (i % 2)) % col_devices) for i in range(col_devices)]
    )
    beside = lax.ppermute(beside, "col", [(i, i ^ 1) for i in range(col_devices)])
    ends = jax.ShapeDtypeStruct((2 * half_rows + (tiles - 2) * DEPTH, TILE), jnp.bfloat16)
    spins, given, kept = call(
        side_kernel,
        [smem, vmem, vmem, vmem, anywhere],
        [jax.ShapeDtypeStruct((DEPTH, columns), jnp.int32), ends, ends],
        [
            pltpu.VMEM((2, rows, TILE), jnp.bfloat16),
            pltpu.VMEM((2, DEPTH, columns), jnp.bfloat16),
            pltpu.VMEM((DEPTH, columns + 2 * LANES), jnp.int32),
            dma((4,)),
        ],
        10 * rows * columns,
        rows * columns,
        odd,
        joined,
        beside,
        across,
        moments,
    )
    own = [own[0], own[1], given, own[2], own[3], kept]
    mid, far = exchange(given, kept)

    spins_out = pl.pallas_call(
        spell_kernel,
        in_specs=[vmem],
        out_specs=anywhere,
        out_shape=jax.ShapeDtypeStruct((rows, columns), jnp.float32),
        scratch_shapes=[pltpu.VMEM((rows, columns), jnp.float32), dma((planes,))],
        compiler_params=params(),
        cost_estimate=pl.CostEstimate(
            flops=rows * columns, bytes_accessed=4 * rows * columns, transcendentals=0
        ),
        name="spell",
    )(spins)
    normaliser = 1.0 / math.sqrt(rows * row_devices * columns * col_devices)
    sums = pltpu.VMEM((TILE, R + TILE), jnp.float32)
    folded = jax.ShapeDtypeStruct((8, R + LANES), jnp.float32)
    work = rows * columns * columns
    base = call(own_kernel, [vmem] * 6, folded, [sums], work, 2 * rows * columns, *own)
    base = call(
        early_kernel,
        [smem] + [vmem] * 7,
        folded,
        [sums],
        work // 2,
        2 * rows * columns,
        odd,
        own[3],
        own[4],
        *got,
        base,
    )
    partial_sums = call(
        functools.partial(late_kernel, normaliser),
        [smem] + [vmem] * 10,
        jax.ShapeDtypeStruct((devices, 1, R // devices), jnp.float32),
        [sums],
        work // 2,
        2 * rows * columns,
        odd,
        own[3],
        own[4],
        own[5],
        got[0],
        got[1],
        mid,
        got[2],
        got[3],
        far,
        base,
    )
    shares = lax.all_to_all(partial_sums, ("row", "col"), 0, 0, tiled=True)
    return spins_out, jnp.sum(shares, axis=(0, 1))


def solution(mesh):
    placed = (P("row", "col"), P(None, "row", "col"), P("row", "col"), P())
    return jax.shard_map(
        on_device,
        mesh=mesh,
        in_specs=placed,
        out_specs=(P("row", "col"), P(("row", "col"))),
        check_vma=False,
    )
```

```python
import functools
import math

import jax
import jax.numpy as jnp
from jax import lax
from jax.experimental import pallas as pl
from jax.experimental.pallas import tpu as pltpu
from jax.sharding import PartitionSpec as P

R = 2048
SWEEPS = 2
DEPTH = 32
LANES = 128
TILE = 256
PER_STEP = 2
MIDDLE = 5
WORDS = 1 + 2 * SWEEPS


def params(**more):
    return pltpu.CompilerParams(vmem_limit_bytes=48 << 20, **more)


def fetch(step, spins_hbm, draws_hbm, spins_buf, draws_buf, sems, row, at, count):
    copies = [
        pltpu.make_async_copy(
            spins_hbm.at[pl.ds(row, count)], spins_buf.at[pl.ds(at, count)], sems.at[step, 0]
        )
    ]
    for k in range(SWEEPS):
        copies.append(
            pltpu.make_async_copy(
                draws_hbm.at[k, pl.ds(row, count)],
                draws_buf.at[k, pl.ds(at, count)],
                sems.at[step, 1 + k],
            )
        )
    return copies


def pack(bar_ref, words_ref, spins_buf, draws_buf, planes, at, fresh):
    columns = words_ref.shape[2]
    for left in range(0, columns, TILE):
        lanes = pl.ds(left, TILE)
        if fresh:
            words = [jnp.zeros((DEPTH, TILE), jnp.int32)] * WORDS
        else:
            words = [words_ref[w, :, lanes] for w in range(WORDS)]
        for i, plane in enumerate(planes):
            bit = 1 << (plane + 1)
            rows = pl.ds(at + i * DEPTH, DEPTH)
            words[0] = words[0] | (spins_buf[rows, lanes] << (plane + 1))
            for k in range(SWEEPS):
                draw = draws_buf[k, rows, lanes]
                for c in range(2):
                    word = words[1 + 2 * k + c]
                    words[1 + 2 * k + c] = jnp.where(draw < bar_ref[c], word | bit, word)
        for w, word in enumerate(words):
            words_ref[w, :, lanes] = word


def groups_of(planes, size):
    return [planes[i : i + size] for i in range(0, len(planes), size)]


def strips(parts):
    return jnp.concatenate(parts, axis=0).astype(jnp.float32).astype(jnp.bfloat16)


def codes(bits):
    return [bits[0]] + [bits[1 + 2 * k] + 2 * bits[2 + 2 * k] for k in range(SWEEPS)]


def unstrips(ref, height):
    parts = [
        ref[k * height : (k + 1) * height, :].astype(jnp.float32).astype(jnp.int32)
        for k in range(1 + SWEEPS)
    ]
    bits = [parts[0]]
    for code in parts[1:]:
        bits += [code & 1, code >> 1]
    return bits


def spread(word):
    for shift in (4, 8, 16, 32, 64):
        word = word | pltpu.roll(word, shift, 1)
    return word


def sweeps_of(words):
    spins = words[0]
    width = spins.shape[1]
    row = lax.broadcasted_iota(jnp.int32, spins.shape, 0)
    parity = (row + lax.broadcasted_iota(jnp.int32, spins.shape, 1)) & 1
    for k in range(SWEEPS):
        for colour in range(2):
            up = pltpu.roll(spins, 1, 0)
            up = jnp.where(row == 0, up << 1, up)
            down = pltpu.roll(spins, DEPTH - 1, 0)
            down = jnp.where(row == DEPTH - 1, down >> 1, down)
            a, b = up ^ spins, down ^ spins
            c, d = pltpu.roll(spins, 1, 1) ^ spins, pltpu.roll(spins, width - 1, 1) ^ spins
            either, other = a | b, c | d
            some = either | other
            several = (a & b) | (c & d) | (either & other)
            flips = several | (some & words[1 + 2 * k]) | (words[2 + 2 * k] & ~some)
            spins = jnp.where(parity == colour, spins ^ flips, spins)
    return spins


def weigh(spins, moments, plane):
    up = (spins & (jnp.int32(1) << (plane + 1))) != 0
    return jnp.where(up, 1.0, -1.0).astype(jnp.bfloat16) * moments


def select(odd, when_odd, when_even):
    return jnp.where(odd == 1, when_odd, when_even)


def fill(refs, odd, planes_of, moments_of, spins_of):
    for ref, lower in zip(refs, (1 - odd, odd)):
        for i, plane in enumerate(planes_of(lower)):
            for t in range(ref.shape[0]):
                ref[t, i * DEPTH : (i + 1) * DEPTH, :] = weigh(
                    spins_of(t), moments_of(lower, i, t), plane
                )


def middle_kernel(
    odd_ref,
    bar_ref,
    spins_hbm,
    draws_hbm,
    moments_hbm,
    words_ref,
    last_ref,
    first_ref,
    given_ref,
    kept_ref,
    spins_buf,
    draws_buf,
    edge_spins,
    edge_draws,
    moments_buf,
    final_ref,
    bar_smem,
    sems,
    edge_sems,
):
    rows, columns = spins_hbm.shape
    half = rows // DEPTH // 2
    planes = list(range(half - MIDDLE - 1, half + MIDDLE + 1))
    top = planes[0] * DEPTH
    groups = groups_of(planes, 2 * PER_STEP)
    size = 2 * PER_STEP * DEPTH
    edges = [
        fetch(s, spins_hbm, draws_hbm, edge_spins, edge_draws, edge_sems, row, 8 * s, 8)
        for s, row in enumerate((rows - 8, 0))
    ]
    copies = [
        fetch(
            g,
            spins_hbm,
            draws_hbm,
            spins_buf,
            draws_buf,
            sems,
            top + g * size,
            g * size,
            len(group) * DEPTH,
        )
        for g, group in enumerate(groups)
    ]
    weights = pltpu.make_async_copy(
        moments_hbm.at[pl.ds((half - MIDDLE) * DEPTH, 2 * MIDDLE * DEPTH)],
        moments_buf,
        edge_sems.at[2, 0],
    )
    bars = pltpu.make_async_copy(bar_ref, bar_smem, edge_sems.at[2, 1])
    for copy in [bars] + sum(edges + copies, []) + [weights]:
        copy.start()
    bars.wait()
    bar_ref = bar_smem
    for s, ref in enumerate((last_ref, first_ref)):
        for copy in edges[s]:
            copy.wait()
        parts = [edge_spins[8 * s : 8 * s + 8, :]]
        for k in range(SWEEPS):
            draw = edge_draws[k, 8 * s : 8 * s + 8, :]
            one = (draw < bar_ref[0]).astype(jnp.int32)
            parts.append(one + 2 * (draw < bar_ref[1]).astype(jnp.int32))
        ref[...] = strips(parts + [jnp.zeros_like(parts[0])])
    for g, group in enumerate(groups):
        for copy in copies[g]:
            copy.wait()
        pack(bar_ref, words_ref, spins_buf, draws_buf, group, g * size, g == 0)
    inner = slice(LANES, columns - LANES)
    final_ref[:, inner] = sweeps_of([words_ref[w, :, inner] for w in range(WORDS)])
    weights.wait()
    for ref, lower in ((given_ref, 1 - odd_ref[0]), (kept_ref, odd_ref[0])):
        for i in range(MIDDLE):
            plane = half - MIDDLE + MIDDLE * lower + i
            at = pl.ds(pl.multiple_of((MIDDLE * lower + i) * DEPTH, DEPTH), DEPTH)
            for t in range(ref.shape[0]):
                lanes = pl.ds((t + 1) * TILE, TILE)
                ref[t, i * DEPTH : (i + 1) * DEPTH, :] = weigh(
                    final_ref[:, lanes], moments_buf[at, lanes], plane
                )


def outer_kernel(
    odd_ref,
    bar_hbm,
    spins_hbm,
    draws_hbm,
    moments_hbm,
    middle_ref,
    words_ref,
    given_ref,
    kept_ref,
    given_rest_ref,
    kept_rest_ref,
    spins_buf,
    draws_buf,
    moments_buf,
    final_ref,
    bar_ref,
    sems,
    more_sems,
):
    rows, columns = spins_hbm.shape
    planes = rows // DEPTH
    side = planes // 2 - MIDDLE - 1
    outer = list(range(side)) + list(range(planes - side, planes))
    bars = pltpu.make_async_copy(bar_hbm, bar_ref, more_sems.at[2])
    bars.start()
    copies = []
    for g, plane in enumerate(outer):
        copies.append(
            fetch(
                g,
                spins_hbm,
                draws_hbm,
                spins_buf,
                draws_buf,
                sems,
                plane * DEPTH,
                g * DEPTH,
                DEPTH,
            )
        )
        for copy in copies[-1]:
            copy.start()
    weights = [
        pltpu.make_async_copy(
            moments_hbm.at[pl.ds(row, side * DEPTH)], moments_buf.at[s], more_sems.at[s]
        )
        for s, row in enumerate((DEPTH, rows - (side + 1) * DEPTH))
    ]
    for copy in weights:
        copy.start()
    words_ref[...] = middle_ref[...]
    bars.wait()
    for g in range(0, len(outer), PER_STEP):
        group = outer[g : g + PER_STEP]
        for copy in sum(copies[g : g + PER_STEP], []):
            copy.wait()
        pack(bar_ref, words_ref, spins_buf, draws_buf, group, g * DEPTH, False)
    inner = slice(LANES, columns - LANES)
    final_ref[:, inner] = sweeps_of([words_ref[w, :, inner] for w in range(WORDS)])
    for copy in weights:
        copy.wait()
    for refs, first, count in (
        ((given_ref, kept_ref), 0, side - 1),
        ((given_rest_ref, kept_rest_ref), side - 1, 1),
    ):
        fill(
            refs,
            odd_ref[0],
            lambda lower: [1 + first + i + (planes - side - 2) * lower for i in range(count)],
            lambda lower, i, t: moments_buf[
                lower,
                (first + i) * DEPTH : (first + i + 1) * DEPTH,
                pl.ds((t + 1) * TILE, TILE),
            ],
            lambda t: final_ref[:, pl.ds((t + 1) * TILE, TILE)],
        )


def join_kernel(odd_ref, words_ref, above_ref, below_ref, joined_ref, beside_ref, across_ref, *, planes):
    columns = words_ref.shape[2]
    above, below = unstrips(above_ref, 8), unstrips(below_ref, 8)
    joined_ref[...] = words_ref[...]
    for w in range(WORDS):
        joined_ref[w, DEPTH - 8 :, :] = words_ref[w, DEPTH - 8 :, :] | above[w]
        joined_ref[w, :8, :] = words_ref[w, :8, :] | (below[w] << (planes + 1))
    lane = lax.broadcasted_iota(jnp.int32, (DEPTH, LANES), 1)
    sent = []
    for at, held in ((columns - LANES, lane >= LANES - 4), (0, lane < 4)):
        bits = []
        for w in range(WORDS):
            edge = jnp.where(held, joined_ref[w, :, at : at + LANES], 0)
            bits.append((spread(edge) >> (lane // 4)) & 1)
        sent.append(jnp.concatenate(codes(bits), axis=0).astype(jnp.float32))
    odd = odd_ref[0]
    beside_ref[...] = select(odd, sent[1], sent[0]).astype(jnp.bfloat16)
    across_ref[...] = select(odd, sent[0], sent[1]).astype(jnp.bfloat16)


def side_kernel(
    odd_ref,
    joined_ref,
    beside_ref,
    across_ref,
    moments_hbm,
    spins_ref,
    given_ref,
    kept_ref,
    tile_moments,
    row_moments,
    final_ref,
    sems,
):
    rows, columns = moments_hbm.shape
    planes = rows // DEPTH
    half = planes // 2
    side = half - MIDDLE
    weights = [
        pltpu.make_async_copy(
            moments_hbm.at[:, pl.ds(at, TILE)], tile_moments.at[s], sems.at[s]
        )
        for s, at in enumerate((0, columns - TILE))
    ] + [
        pltpu.make_async_copy(
            moments_hbm.at[pl.ds(at, DEPTH)], row_moments.at[s], sems.at[2 + s]
        )
        for s, at in enumerate((0, rows - DEPTH))
    ]
    for copy in weights:
        copy.start()
    lane = lax.broadcasted_iota(jnp.int32, (DEPTH, LANES), 1)
    odd = odd_ref[0]
    words = []
    for w, halos in enumerate(zip(unstrips(beside_ref, DEPTH), unstrips(across_ref, DEPTH))):
        before, after = select(odd, *halos), select(odd, *halos[::-1])
        words.append(
            jnp.concatenate(
                [spread(before << (lane // 4)), joined_ref[w], spread(after << (lane // 4))],
                axis=1,
            )
        )
    final_ref[...] = sweeps_of(words)
    spins_ref[...] = final_ref[:, LANES : LANES + columns]
    for copy in weights:
        copy.wait()
    odd = odd_ref[0]
    ends = (0, columns - TILE)
    for ref, lower in ((given_ref, 1 - odd), (kept_ref, odd)):
        for i in range(half):
            if i < side - 1:
                plane = 1 + i + (planes - side - 1) * lower
            elif i < half - 1:
                plane = 1 + i + MIDDLE * lower
            else:
                plane = (planes - 1) * lower
            at = pl.ds(pl.multiple_of(plane * DEPTH, DEPTH), DEPTH)
            for s, left in enumerate(ends):
                row = (s * half + i) * DEPTH
                ref[row : row + DEPTH, :] = weigh(
                    final_ref[:, LANES + left : LANES + left + TILE], tile_moments[s, at, :], plane
                )
        for t in range(1, columns // TILE - 1):
            row = (2 * half + t - 1) * DEPTH
            ref[row : row + DEPTH, :] = weigh(
                final_ref[:, LANES + t * TILE : LANES + (t + 1) * TILE],
                row_moments[lower, :, t * TILE : (t + 1) * TILE],
                (planes - 1) * lower,
            )


def spell_kernel(spins_ref, out_hbm, out_buf, sems):
    columns = spins_ref.shape[1]
    copies = []
    for plane in range(out_hbm.shape[0] // DEPTH):
        rows = pl.ds(plane * DEPTH, DEPTH)
        for left in range(0, columns, TILE):
            lanes = pl.ds(left, TILE)
            up = (spins_ref[:, lanes] & (1 << (plane + 1))) != 0
            out_buf[rows, lanes] = jnp.where(up, 1.0, -1.0)
        copies.append(pltpu.make_async_copy(out_buf.at[rows], out_hbm.at[rows], sems.at[plane]))
        copies[-1].start()
    for copy in copies:
        copy.wait()


def gram(left, right):
    return lax.dot_general(
        left, right, (((0,), (0,)), ((), ())), preferred_element_type=jnp.float32
    )


def stack(refs, first, last):
    return jnp.concatenate(
        [ref[first:last].reshape((last - first) * ref.shape[1], TILE) for ref in refs], axis=0
    )


def fold(sums_ref):
    width = R + LANES
    value = sums_ref[:LANES, :width] + sums_ref[LANES:, LANES : LANES + width]
    height = LANES // 2
    while height >= 8:
        value = value[:height] + pltpu.roll(value[height:], width - height, 1)
        height //= 2
    return value


def edge_rows(ends, tiles, first, last):
    start = ends.shape[0] - (tiles - 2) * DEPTH
    return ends[start + (first - 1) * DEPTH : start + (last - 1) * DEPTH, :]


def tile(block, t):
    parts, ends, spans, edges = block
    tiles = parts[0].shape[0] + 2
    height = (ends.shape[0] - (tiles - 2) * DEPTH) // 2
    if t in (0, tiles - 1):
        base = min(t, 1) * height
        return jnp.concatenate([ends[base + a : base + b, :] for a, b in spans], axis=0)
    rows = [part[t - 1] for part in parts]
    if edges:
        rows.append(edge_rows(ends, tiles, t, t + 1))
    return jnp.concatenate(rows, axis=0)


def tiles_of(block, places):
    return jnp.concatenate([tile(block, t) for t in places], axis=0)


def whole(parts):
    low, rest, high, ends = parts
    return (low, rest, high), ends, ((0, low.shape[1] + rest.shape[1] + high.shape[1] + DEPTH),), True


def without_rest(parts):
    low, rest, high, ends = parts
    held = low.shape[1] + rest.shape[1]
    return (low, high), ends, ((0, low.shape[1]), (held, held + high.shape[1] + DEPTH)), True


def rest_only(parts):
    low, rest, _, ends = parts
    return (rest,), ends, ((low.shape[1], low.shape[1] + rest.shape[1]),), False


def own_kernel(*refs):
    parts, (out_ref, sums_ref) = refs[:-2], refs[-2:]
    blocks = (whole(parts[:4]), whole(parts[4:]))
    tiles = parts[0].shape[0] + 2
    for n in range(tiles):
        sums_ref[:, n * TILE : (n + 1) * TILE] = sum(
            gram(tiles_of(block, range(tiles - n)), tiles_of(block, range(n, tiles)))
            for block in blocks
        )
    sums_ref[:, tiles * TILE :] = jnp.zeros((TILE, TILE), jnp.float32)
    out_ref[...] = fold(sums_ref)


def by_side(odd_ref, own, mid, far, run):
    @pl.when(odd_ref[0] == 0)
    def _():
        run(((own, mid), (mid, far)))

    @pl.when(odd_ref[0] == 1)
    def _():
        run(((far, mid), (mid, own)))


def early_kernel(odd_ref, *refs):
    (base_ref, out_ref, sums_ref) = refs[-3:]
    tiles = refs[0].shape[0]
    sums_ref[:, : 3 * TILE] = jnp.zeros((TILE, 3 * TILE), jnp.float32)

    def run(pairs):
        for n in range(1, tiles + 1):
            sums_ref[:, (n + 2) * TILE : (n + 3) * TILE] = sum(
                gram(stack(left, tiles - n, tiles), stack(right, 0, n)) for left, right in pairs
            )

    by_side(odd_ref, refs[0:2], refs[2:4], refs[4:6], run)
    out_ref[...] = fold(sums_ref) + base_ref[...]


def late_kernel(odd_ref, *refs):
    (base_ref, out_ref, sums_ref) = refs[-3:]
    tiles = refs[0].shape[0] + 2
    sums_ref[:, :TILE] = jnp.zeros((TILE, TILE), jnp.float32)

    def run(pairs):
        pairs = [tuple(without_rest(part) for part in pair) for pair in pairs]
        for n in range(1, tiles + 1):
            places = [(tiles - 1, n - 1)] + ([(tiles - n, 0)] if n > 1 else [])
            total = 0.0
            for left, right in pairs:
                lefts, rights = [tile(left, t) for t, _ in places], [tile(right, q) for _, q in places]
                if n > 2:
                    lefts.append(edge_rows(left[1], tiles, tiles + 1 - n, tiles - 1))
                    rights.append(edge_rows(right[1], tiles, 1, n - 1))
                total += gram(jnp.concatenate(lefts, axis=0), jnp.concatenate(rights, axis=0))
            sums_ref[:, n * TILE : (n + 1) * TILE] = total

    by_side(odd_ref, refs[0:4], refs[4:8], refs[8:12], run)
    out_ref[...] = fold(sums_ref) + base_ref[...]


def last_kernel(scale, odd_ref, *refs):
    (base_ref, out_ref, sums_ref) = refs[-3:]
    tiles = refs[0].shape[0] + 2
    sums_ref[:, :TILE] = jnp.zeros((TILE, TILE), jnp.float32)

    def run(pairs):
        pairs = [tuple(rest_only(part) for part in pair) for pair in pairs]
        for n in range(1, tiles + 1):
            sums_ref[:, n * TILE : (n + 1) * TILE] = gram(
                jnp.concatenate(
                    [tiles_of(left, range(tiles - n, tiles)) for left, _ in pairs], axis=0
                ),
                jnp.concatenate([tiles_of(right, range(n)) for _, right in pairs], axis=0),
            )

    by_side(odd_ref, refs[0:4], refs[4:8], refs[8:12], run)
    value = fold(sums_ref) + base_ref[...]
    for height in (4, 2, 1):
        value = value + pltpu.roll(pltpu.roll(value, value.shape[1] - height, 1), 8 - height, 0)
    value = value[:1] * scale
    share = out_ref.shape[2]
    for d in range(out_ref.shape[0]):
        out_ref[d] = value[:, d * share : (d + 1) * share]


def on_device(spins_up, uniforms, moments, accept_bar):
    rows, columns = spins_up.shape
    planes, tiles = rows // DEPTH, columns // TILE
    half_rows, half = rows // 2, planes // 2
    row_devices, col_devices = lax.axis_size("row"), lax.axis_size("col")
    devices = row_devices * col_devices
    assert columns == R and col_devices % 2 == 0 and planes % 2 == 0 and planes + 2 <= 26
    vmem = pl.BlockSpec(memory_space=pltpu.VMEM)
    smem = pl.BlockSpec(memory_space=pltpu.SMEM)
    anywhere = pl.BlockSpec(memory_space=pltpu.HBM)
    strip = jax.ShapeDtypeStruct((8 * (2 + SWEEPS), columns), jnp.bfloat16)
    edge = jax.ShapeDtypeStruct((DEPTH * (1 + SWEEPS), LANES), jnp.bfloat16)
    words_shape = jax.ShapeDtypeStruct((WORDS, DEPTH, columns), jnp.int32)
    dma = pltpu.SemaphoreType.DMA
    odd = (lax.axis_index("col") % 2).reshape(1)
    moments = pltpu.with_memory_space_constraint(moments, pltpu.HBM)
    accept_bar = pltpu.with_memory_space_constraint(accept_bar, pltpu.HBM)

    def message(count, height):
        return jax.ShapeDtypeStruct((count, height, TILE), jnp.bfloat16)

    def ring(size, step):
        return [(i, (i + step) % size) for i in range(size)]

    def exchange(given, kept):
        beside = [(i, i ^ 1) for i in range(col_devices)]
        beyond = [(i, (i - 2 + 4 * (i % 2)) % col_devices) for i in range(col_devices)]
        return lax.ppermute(given, "col", beside), lax.ppermute(kept, "col", beyond)

    def call(kernel, specs, shapes, scratch, flops, moved, *operands):
        return pl.pallas_call(
            kernel,
            in_specs=specs,
            out_specs=jax.tree.map(lambda _: vmem, shapes),
            out_shape=shapes,
            scratch_shapes=scratch,
            compiler_params=params(),
            cost_estimate=pl.CostEstimate(flops=flops, bytes_accessed=moved, transcendentals=0),
        )(*operands)

    packed = (2 * MIDDLE + 2) * DEPTH
    remaining = rows - packed
    side = half - MIDDLE - 1
    middle = message(tiles - 2, MIDDLE * DEPTH)
    words, last, leading, given, kept = call(
        middle_kernel,
        [smem, anywhere, anywhere, anywhere, anywhere],
        [words_shape, strip, strip, middle, middle],
        [
            pltpu.VMEM((packed, columns), jnp.int32),
            pltpu.VMEM((SWEEPS, packed, columns), jnp.float32),
            pltpu.VMEM((16, columns), jnp.int32),
            pltpu.VMEM((SWEEPS, 16, columns), jnp.float32),
            pltpu.VMEM((2 * MIDDLE * DEPTH, columns), jnp.bfloat16),
            pltpu.VMEM((DEPTH, columns), jnp.int32),
            pltpu.SMEM((2,), jnp.float32),
            dma((pl.cdiv(2 * MIDDLE + 2, 2 * PER_STEP), 1 + SWEEPS)),
            dma((3, 1 + SWEEPS)),
        ],
        40 * packed * columns,
        4 * (1 + SWEEPS) * packed * columns,
        odd,
        accept_bar,
        spins_up,
        uniforms,
        moments,
    )
    own = [given, kept]
    got = [*exchange(given, kept)]
    above = lax.ppermute(last, "row", ring(row_devices, 1))
    below = lax.ppermute(leading, "row", ring(row_devices, -1))
    low, rest = message(tiles - 2, (side - 1) * DEPTH), message(tiles - 2, DEPTH)
    words, given, kept, given_rest, kept_rest = call(
        outer_kernel,
        [smem, anywhere, anywhere, anywhere, anywhere, vmem],
        [words_shape, low, low, rest, rest],
        [
            pltpu.VMEM((remaining, columns), jnp.int32),
            pltpu.VMEM((SWEEPS, remaining, columns), jnp.float32),
            pltpu.VMEM((2, side * DEPTH, columns), jnp.bfloat16),
            pltpu.VMEM((DEPTH, columns), jnp.int32),
            pltpu.SMEM((2,), jnp.float32),
            dma((remaining // DEPTH, 1 + SWEEPS)),
            dma((3,)),
        ],
        40 * remaining * columns,
        4 * (1 + SWEEPS) * remaining * columns,
        odd,
        accept_bar,
        spins_up,
        uniforms,
        moments,
        words,
    )
    mid, far = exchange(given, kept)
    given, kept = [given, given_rest, own[0]], [kept, kept_rest, own[1]]
    got = [[mid, got[0]], [far, got[1]]]
    joined, beside, across = call(
        functools.partial(join_kernel, planes=planes),
        [smem, vmem, vmem, vmem],
        [words_shape, edge, edge],
        [],
        20 * DEPTH * columns,
        40 * DEPTH * columns,
        odd,
        words,
        above,
        below,
    )
    across = lax.ppermute(
        across, "col", [(i, (i - 1 + 2 * (i % 2)) % col_devices) for i in range(col_devices)]
    )
    beside = lax.ppermute(beside, "col", [(i, i ^ 1) for i in range(col_devices)])
    ends = jax.ShapeDtypeStruct((2 * half_rows + (tiles - 2) * DEPTH, TILE), jnp.bfloat16)
    spins, given_ends, kept_ends = call(
        side_kernel,
        [smem, vmem, vmem, vmem, anywhere],
        [jax.ShapeDtypeStruct((DEPTH, columns), jnp.int32), ends, ends],
        [
            pltpu.VMEM((2, rows, TILE), jnp.bfloat16),
            pltpu.VMEM((2, DEPTH, columns), jnp.bfloat16),
            pltpu.VMEM((DEPTH, columns + 2 * LANES), jnp.int32),
            dma((4,)),
        ],
        10 * rows * columns,
        rows * columns,
        odd,
        joined,
        beside,
        across,
        moments,
    )
    given, kept = given + [given_ends], kept + [kept_ends]
    mid_ends, far_ends = exchange(given_ends, kept_ends)
    mid_rest, far_rest = exchange(given_rest, kept_rest)

    spins_out = pl.pallas_call(
        spell_kernel,
        in_specs=[vmem],
        out_specs=anywhere,
        out_shape=jax.ShapeDtypeStruct((rows, columns), jnp.float32),
        scratch_shapes=[pltpu.VMEM((rows, columns), jnp.float32), dma((planes,))],
        compiler_params=params(),
        cost_estimate=pl.CostEstimate(
            flops=rows * columns, bytes_accessed=4 * rows * columns, transcendentals=0
        ),
        name="spell",
    )(spins)
    normaliser = 1.0 / math.sqrt(rows * row_devices * columns * col_devices)
    sums = pltpu.VMEM((TILE, R + TILE), jnp.float32)
    folded = jax.ShapeDtypeStruct((8, R + LANES), jnp.float32)
    work = rows * columns * columns
    base = call(own_kernel, [vmem] * 8, folded, [sums], work, 2 * rows * columns, *given, *kept)
    base = call(
        early_kernel,
        [smem] + [vmem] * 7,
        folded,
        [sums],
        work // 2,
        2 * rows * columns,
        odd,
        kept[0],
        kept[2],
        *got[0],
        *got[1],
        base,
    )
    base = call(
        late_kernel,
        [smem] + [vmem] * 13,
        folded,
        [sums],
        work // 2,
        2 * rows * columns,
        odd,
        *kept,
        got[0][0],
        given_rest,
        got[0][1],
        mid_ends,
        got[1][0],
        kept_rest,
        got[1][1],
        far_ends,
        base,
    )
    partial_sums = call(
        functools.partial(last_kernel, normaliser),
        [smem] + [vmem] * 13,
        jax.ShapeDtypeStruct((devices, 1, R // devices), jnp.float32),
        [sums],
        work // 8,
        rows * columns,
        odd,
        *kept,
        got[0][0],
        mid_rest,
        got[0][1],
        mid_ends,
        got[1][0],
        far_rest,
        got[1][1],
        far_ends,
        base,
    )
    shares = lax.all_to_all(partial_sums, ("row", "col"), 0, 0, tiled=True)
    return spins_out, jnp.sum(shares, axis=(0, 1))


def solution(mesh):
    placed = (P("row", "col"), P(None, "row", "col"), P("row", "col"), P())
    return jax.shard_map(
        on_device,
        mesh=mesh,
        in_specs=placed,
        out_specs=(P("row", "col"), P(("row", "col"))),
        check_vma=False,
    )
```
